32 devices in a mesh: groups: 2 (over x), ctx: 8 (over z, y), tp: 2 (over core).
Axes of the slice: x: 2, y: 2, z: 4, core: 2. Of those that a mesh axis runs over, the one named last changes fastest.
Arguments:
- tokens: bfloat16 [8192, 2048], P(('groups', 'ctx')), parts along dimension 0, may hold values from -6 to 6
- weight: bfloat16 [2048, 3, 2048], P('ctx', None, 'tp'), may hold values from -0.125 to 0.125
- adapter_a: bfloat16 [2048, 16], replicated, may hold values from -2.390625 to 2.390625
- adapter_b: bfloat16 [16, 3, 2048], P(None, None, 'tp'), may hold values from -2.390625 to 2.390625
- short_filter: float32 [7, 3, 2048], P(None, None, 'tp'), may hold values from -1.8 to 1.8
- long_filter: float32 [128, 2048], P(None, 'tp'), may hold values from -0.54 to 0.54
- skip_gain: float32 [2048], P('tp'), may hold values from -4.2 to 4.2
- cotangent: bfloat16 [8192, 2048], P(('groups', 'ctx'), 'tp'), parts along dimension 0, may hold values from -6 to 6
Outputs:
- mixed: bfloat16 [8192, 2048], P(('groups', 'ctx'), 'tp'), parts along dimension 0
- grad_tokens: bfloat16 [8192, 2048], P(('groups', 'ctx'), 'tp'), parts along dimension 0
- grad_a: float32 [4096, 16], P('groups'), parts along dimension 0
- grad_b: float32 [32, 3, 2048], P('groups', None, 'tp'), parts along dimension 0
The draws below stay inside these ranges and needn't reach their ends.
There are 2 independent parts, one for each index of `groups`. The reference program is written for one: setup_inputs(seed, part) draws one part's arguments, and reference() takes and returns one part's arrays. A program takes and returns all parts, laid end to end along the dimension named above; an argument that names none is the same for every part. Nothing has to cross between parts.
All inputs are finite; a program needn't handle non-finite values.
Results may differ from the reference program's by a relative error of at most 0.0093.
Values may be sent and summed in bfloat16 or wider, within the bound.
A program may use at most 128 MiB of HBM per device.

```python
import math
import jax
import jax.numpy as jnp
from jax import lax

D = 2048
R = 16
LONG = 128
SHORT = 7
TOK_DEV = 512
TOKENS = 4096
CH = 2048


def shard_levels(stream_key, dims, pieces, least, high):
    def one(axis_at, shards_of):
        heights = jax.random.uniform(jax.random.fold_in(jax.random.fold_in(stream_key, 6), axis_at), (shards_of,), jnp.float32, least / len(pieces), high / len(pieces))
        return jnp.repeat(jnp.exp(heights), dims[axis_at] // shards_of).reshape((-1,) + (1,) * (len(dims) - axis_at - 1))

    gain = one(*pieces[0])
    for cut in pieces[1:]:
        gain = gain * one(*cut)
    return gain


def noise(stream_key, dims, deviation, reach, split=(), held_as=jnp.bfloat16):
    values = jax.random.normal(stream_key, dims, jnp.float32) * deviation
    if len(split) > 0:
        values = shard_levels(stream_key, dims, split, -0.22, 0.18) * values
    return jnp.clip(values, min=-reach, max=reach).astype(held_as)


def setup_inputs(seed: int = 0, part: int = 0) -> dict:
    key_list = jax.random.split(jax.random.key(seed), 9)
    part_splits = jax.random.split(jax.random.fold_in(key_list[8], part), 9)
    return {
        "tokens": noise(part_splits[0], (TOKENS, D), 1.0, 6.0, ((0, 8),)),
        "weight": noise(key_list[1], (D, 3, CH), D ** -0.5, 0.125, ((0, 8), (2, 2))),
        "adapter_a": noise(key_list[2], (D, R), 0.4, 2.390625),
        "adapter_b": noise(key_list[3], (R, 3, CH), 0.4, 2.390625, ((2, 2),)),
        "short_filter": noise(key_list[4], (SHORT, 3, CH), 0.3, 1.8, ((2, 2),), jnp.float32),
        "long_filter": noise(key_list[5], (LONG, CH), 0.09, 0.54, ((1, 2),), jnp.float32),
        "skip_gain": noise(key_list[6], (CH,), 0.7, 4.2, ((0, 2),), jnp.float32),
        "cotangent": noise(part_splits[7], (TOKENS, CH), 1.0, 6.0, ((0, 8), (1, 2))),
    }


adapter_scale = 0.03125

def causal(signal, filter_taps):
    taps = filter_taps.shape[0]
    out_len = signal.shape[0] - taps + 1
    start_acc = jnp.zeros((out_len, signal.shape[1]), jnp.float32)

    def add_tap(index, acc):
        piece = lax.dynamic_slice_in_dim(signal, (taps - 1 - index).astype(jnp.int32), out_len, 0)
        return acc + filter_taps[index] * piece
    return lax.fori_loop(0, taps, add_tap, start_acc)

def anticausal(signal, filter_taps):
    taps = filter_taps.shape[0]
    out_len = signal.shape[0] - taps + 1
    start_acc = jnp.zeros((out_len, signal.shape[1]), jnp.float32)

    def add_tap(index, acc):
        piece = lax.dynamic_slice_in_dim(signal, jnp.asarray(index).astype(jnp.int32), out_len, 0)
        return acc + filter_taps[index] * piece
    return lax.fori_loop(0, taps, add_tap, start_acc)

def reference(tokens, weight, adapter_a, adapter_b, short_filter, long_filter, skip_gain, cotangent):
    channels = weight.shape[2]
    adapter_rank = adapter_a.shape[1]
    short_taps = short_filter.shape[0]
    long_taps = long_filter.shape[0]
    seq_total = tokens.shape[0]
    feature_count = tokens.shape[1]
    block_count = seq_total // TOK_DEV
    delta_w = jnp.dot(adapter_a, adapter_b.reshape(adapter_rank, 3 * channels), preferred_element_type=jnp.float32)
    merged = (weight.reshape(weight.shape[0], 3 * channels).astype(jnp.float32) + adapter_scale * delta_w).astype(jnp.bfloat16)

    def forward_rows(rows):
        return jnp.dot(rows, merged, preferred_element_type=jnp.float32).astype(jnp.bfloat16)
    packed = lax.map(forward_rows, tokens.reshape(block_count, TOK_DEV, feature_count)).reshape(seq_total, 3 * channels)
    short_flat = short_filter.reshape(short_taps, 3 * channels)
    padded = jnp.concatenate([jnp.zeros((short_taps - 1, 3 * channels), jnp.float32), packed.astype(jnp.float32)], axis=0)
    short_out = causal(padded, short_flat)
    query = short_out[:, :channels]
    keyed = short_out[:, channels:2 * channels]
    valued = short_out[:, 2 * channels:]
    gated = (keyed * valued).astype(jnp.bfloat16)
    gated_pad = jnp.concatenate([jnp.zeros((long_taps - 1, channels), jnp.float32), gated.astype(jnp.float32)], axis=0)
    filtered = causal(gated_pad, long_filter) + skip_gain * gated.astype(jnp.float32)
    mixed = (query * filtered).astype(jnp.bfloat16)
    cot_f = cotangent.astype(jnp.float32)
    grad_filtered = (cot_f * query).astype(jnp.bfloat16)
    back_pad = jnp.concatenate([grad_filtered.astype(jnp.float32), jnp.zeros((long_taps - 1, channels), jnp.float32)], axis=0)
    grad_gated = anticausal(back_pad, long_filter) + skip_gain * grad_filtered.astype(jnp.float32)
    grad_short = jnp.concatenate([cot_f * filtered, grad_gated * valued, grad_gated * keyed], axis=1).astype(jnp.bfloat16)
    short_pad = jnp.concatenate([grad_short.astype(jnp.float32), jnp.zeros((short_taps - 1, 3 * channels), jnp.float32)], axis=0)
    grad_packed = anticausal(short_pad, short_flat).astype(jnp.bfloat16)

    def backward_rows(rows):
        return lax.dot_general(rows, merged, (((1,), (1,)), ((), ())), preferred_element_type=jnp.float32).astype(jnp.bfloat16)
    grad_tokens = lax.map(backward_rows, grad_packed.reshape(block_count, TOK_DEV, 3 * channels)).reshape(seq_total, feature_count)
    factor = adapter_scale / math.sqrt(seq_total)
    projected = jnp.dot(tokens, adapter_a, preferred_element_type=jnp.float32).astype(jnp.bfloat16)
    grad_b = lax.dot_general(projected, grad_packed, (((0,), (0,)), ((), ())), preferred_element_type=jnp.float32) * factor
    through_b = lax.dot_general(grad_packed, adapter_b.reshape(adapter_rank, 3 * channels), (((1,), (1,)), ((), ())), preferred_element_type=jnp.float32).astype(jnp.bfloat16)
    grad_a = lax.dot_general(tokens, through_b, (((0,), (0,)), ((), ())), preferred_element_type=jnp.float32) * factor
    return (mixed, grad_tokens, grad_a, grad_b.reshape(adapter_rank, 3, channels))
```

```python
import functools
import math

import jax
import jax.numpy as jnp
from jax import lax
from jax.experimental import pallas as pl
from jax.experimental.pallas import tpu as pltpu
from jax.sharding import PartitionSpec as P

adapter_scale = 0.03125
LANES = 128
SUB = 8
BLOCK = 16
CHUNK = 32


def shifted(value, axis, steps):
    count = lax.axis_size(axis)
    initial, last = (max(0, -steps), min(count, count - steps))
    return lax.ppermute(value, axis, [(source, source + steps) for source in range(initial, last)])


def tiles(ref, first, count):
    start = first * SUB
    if not isinstance(start, int):
        start = pl.multiple_of(start, SUB)
    return ref[pl.ds(start, count * SUB), :].reshape(count, SUB, LANES)


def put(ref, first, value):
    count = value.shape[0]
    ref[pl.ds(pl.multiple_of(first * SUB, SUB), count * SUB), :] = value.reshape(count * SUB, LANES)


def rounded(value):
    return value.astype(jnp.bfloat16).astype(jnp.float32)


def mixer_kernel(
    rows, halo, packed_ref, cot_ref, short_ref, long_ref, skip_ref, mixed_ref, grad_ref,
    p0, p1, p2, cot, query, keyed, valued, gated, gradf,
):
    channels = SUB * LANES
    short_taps = short_ref.shape[0] // 3
    long_taps = long_ref.shape[0]
    spread = (p0, p1, p2)
    front = halo - long_taps

    @pl.loop(0, (rows + 2 * halo) // BLOCK)
    def _(i):
        at = pl.multiple_of(i * BLOCK, BLOCK)
        for g in range(3):
            for s in range(SUB):
                piece = packed_ref[pl.ds(at, BLOCK), pl.ds(g * channels + s * LANES, LANES)]
                spread[g][pl.ds(at * SUB + s, BLOCK, stride=SUB), :] = piece.astype(jnp.float32)

    @pl.loop(0, (rows + halo) // BLOCK)
    def _(i):
        at = pl.multiple_of(i * BLOCK, BLOCK)
        for s in range(SUB):
            piece = cot_ref[pl.ds(at, BLOCK), pl.ds(s * LANES, LANES)]
            cot[pl.ds(at * SUB + s, BLOCK, stride=SUB), :] = piece.astype(jnp.float32)

    def short(ref, g, first, sign):
        total = None
        for j in range(short_taps):
            term = short_ref[j * 3 + g][None] * tiles(ref, first + sign * j, SUB)
            total = term if total is None else total + term
        return total

    @pl.loop(0, (rows + BLOCK + long_taps) // SUB)
    def _(i):
        at = i * SUB
        key = short(p1, 1, at + front, -1)
        val = short(p2, 2, at + front, -1)
        put(keyed, at, key)
        put(valued, at, val)
        put(gated, at, rounded(key * val))

    @pl.loop(0, (rows + halo) // SUB)
    def _(i):
        at = i * SUB
        que = short(p0, 0, at + halo, -1)
        put(query, at, que)
        put(gradf, at, rounded(que * tiles(cot, at, SUB)))

    zero = tuple(jnp.zeros((SUB, LANES), jnp.float32) for _ in range(BLOCK))

    def long_sum(ref, base, sign):
        def chunk(c, acc):
            acc = list(acc)
            tap0 = c * CHUNK
            origin = base + sign * tap0
            low = origin - (CHUNK - 1) if sign < 0 else origin
            seen = {}

            def at(k):
                if k not in seen:
                    seen[k] = ref[pl.ds(pl.multiple_of((low + k) * SUB, SUB), SUB), :]
                return seen[k]

            for j in range(CHUNK):
                tap = long_ref[tap0 + j]
                for i in range(BLOCK):
                    k = i + (CHUNK - 1) - j if sign < 0 else i + j
                    acc[i] = acc[i] + tap * at(k)
            return tuple(acc)

        return lax.fori_loop(0, long_taps // CHUNK, chunk, zero)

    @pl.loop(0, (rows + BLOCK) // BLOCK)
    def _(b):
        at = b * BLOCK
        skip = skip_ref[...]
        ahead = jnp.stack(long_sum(gated, at + long_taps, -1))
        filtered = ahead + skip[None] * tiles(gated, at + long_taps, BLOCK)
        back = jnp.stack(long_sum(gradf, at, 1))
        grad_gated = back + skip[None] * tiles(gradf, at, BLOCK)
        put(p0, at, rounded(tiles(cot, at, BLOCK) * filtered))
        put(p1, at, rounded(grad_gated * tiles(valued, at + long_taps, BLOCK)))
        put(p2, at, rounded(grad_gated * tiles(keyed, at + long_taps, BLOCK)))
        put(gated, at, tiles(query, at, BLOCK) * filtered)

    results = (query, keyed, valued)

    @pl.loop(0, rows // SUB)
    def _(i):
        at = i * SUB
        for g in range(3):
            put(results[g], at, short(spread[g], g, at, 1))

    @pl.loop(0, rows // BLOCK)
    def _(i):
        at = pl.multiple_of(i * BLOCK, BLOCK)
        for s in range(SUB):
            pick = pl.ds(at * SUB + s, BLOCK, stride=SUB)
            mixed_ref[pl.ds(at, BLOCK), pl.ds(s * LANES, LANES)] = gated[pick, :].astype(jnp.bfloat16)
            for g in range(3):
                grad_ref[pl.ds(at, BLOCK), pl.ds(g * channels + s * LANES, LANES)] = results[g][
                    pick, :
                ].astype(jnp.bfloat16)


def mixer(packed, cot, short_filter, long_filter, skip_gain, rows, halo):
    channels = long_filter.shape[1]
    long_taps = long_filter.shape[0]
    full = (rows + 2 * halo) * SUB
    side = (rows + halo) * SUB
    scratch = [pltpu.VMEM((full, LANES), jnp.float32)] * 3 + [
        pltpu.VMEM((side, LANES), jnp.float32)
    ] * 6
    return pl.pallas_call(
        functools.partial(mixer_kernel, rows, halo),
        out_shape=(
            jax.ShapeDtypeStruct((rows, channels), jnp.bfloat16),
            jax.ShapeDtypeStruct((rows, 3 * channels), jnp.bfloat16),
        ),
        in_specs=[pl.BlockSpec(memory_space=pltpu.VMEM)] * 5,
        out_specs=(pl.BlockSpec(memory_space=pltpu.VMEM),) * 2,
        scratch_shapes=scratch,
        compiler_params=pltpu.CompilerParams(vmem_limit_bytes=52 << 20),
        cost_estimate=pl.CostEstimate(
            flops=4 * rows * channels * (long_taps + 42), bytes_accessed=12 << 20, transcendentals=0
        ),
    )(
        packed,
        cot,
        short_filter.reshape(-1, SUB, LANES),
        long_filter.reshape(long_taps, SUB, LANES),
        skip_gain.reshape(SUB, LANES),
    )


def body(tokens, weight, adapter_a, adapter_b, short_filter, long_filter, skip_gain, cotangent):
    row_count = tokens.shape[0]
    share_rows = weight.shape[0]
    channels = weight.shape[2]
    features = tokens.shape[1]
    adapter_rank = adapter_a.shape[1]
    halo = long_filter.shape[0] + BLOCK
    seq_total = row_count * lax.axis_size("ctx")
    first_row = lax.axis_index("ctx") * share_rows
    before = shifted(tokens[row_count - halo :], "ctx", 1)
    after = shifted(tokens[:halo], "ctx", -1)
    cot_after = shifted(cotangent[:halo], "ctx", -1)
    tokens_ext = jnp.concatenate([before, tokens, after], axis=0)
    cot_ext = jnp.concatenate([cotangent, cot_after], axis=0)
    own_rows = lax.dynamic_slice_in_dim(adapter_a, first_row, share_rows, 0)
    flat_b = adapter_b.reshape(adapter_rank, 3 * channels)
    delta_w = jnp.dot(own_rows, flat_b, preferred_element_type=jnp.float32)
    merged = (
        weight.reshape(share_rows, 3 * channels).astype(jnp.float32) + adapter_scale * delta_w
    ).astype(jnp.bfloat16)
    whole = lax.all_gather(merged, "ctx", axis=0, tiled=True)
    packed = jnp.dot(tokens_ext, whole, preferred_element_type=jnp.float32).astype(jnp.bfloat16)
    mixed, grad_packed = mixer(
        packed, cot_ext, short_filter, long_filter, skip_gain, row_count, halo
    )
    projected = jnp.dot(tokens, adapter_a, preferred_element_type=jnp.float32).astype(jnp.bfloat16)
    part_b = lax.dot_general(
        projected, grad_packed, (((0,), (0,)), ((), ())), preferred_element_type=jnp.float32
    )
    through = lax.dot_general(
        flat_b, grad_packed, (((1,), (1,)), ((), ())), preferred_element_type=jnp.float32
    ).astype(jnp.bfloat16)
    part_a = jnp.dot(through, tokens, preferred_element_type=jnp.float32)
    mine = lax.axis_index("tp")
    spread_b = [jnp.where(mine == k, part_b, 0.0) for k in range(lax.axis_size("tp"))]
    sums = lax.psum(jnp.concatenate([part_a] + spread_b, axis=1), ("ctx", "tp"))
    sum_a = sums[:, :features].T
    sum_b = lax.dynamic_slice_in_dim(sums, features + mine * 3 * channels, 3 * channels, 1)
    partial_grad = lax.dot_general(
        grad_packed, whole, (((1,), (1,)), ((), ())), preferred_element_type=jnp.float32
    )
    grad_tokens = lax.psum_scatter(
        partial_grad.astype(jnp.bfloat16), "tp", scatter_dimension=1, tiled=True
    )
    factor = adapter_scale / math.sqrt(seq_total)
    return (mixed, grad_tokens, sum_a * factor, (sum_b * factor).reshape(adapter_rank, 3, channels))


def solution(mesh):
    return jax.shard_map(
        body,
        mesh=mesh,
        in_specs=(
            P(("groups", "ctx"), None),
            P("ctx", None, "tp"),
            P(),
            P(None, None, "tp"),
            P(None, None, "tp"),
            P(None, "tp"),
            P("tp"),
            P(("groups", "ctx"), "tp"),
        ),
        out_specs=(
            P(("groups", "ctx"), "tp"),
            P(("groups", "ctx"), "tp"),
            P("groups", None),
            P("groups", None, "tp"),
        ),
        check_vma=False,
    )
```

```python
import functools
import math

import jax
import jax.numpy as jnp
from jax import lax
from jax.experimental import pallas as pl
from jax.experimental.pallas import tpu as pltpu
from jax.sharding import PartitionSpec as P

adapter_scale = 0.03125
LANES = 128
SUB = 8
BLOCK = 16
CHUNK = 32


def shifted(value, axis, steps):
    count = lax.axis_size(axis)
    initial, last = (max(0, -steps), min(count, count - steps))
    return lax.ppermute(value, axis, [(source, source + steps) for source in range(initial, last)])


def tiles(ref, first, count):
    start = first * SUB
    if not isinstance(start, int):
        start = pl.multiple_of(start, SUB)
    return ref[pl.ds(start, count * SUB), :].reshape(count, SUB, LANES)


def put(ref, first, value):
    count = value.shape[0]
    ref[pl.ds(pl.multiple_of(first * SUB, SUB), count * SUB), :] = value.reshape(count * SUB, LANES)


def rounded(value):
    return value.astype(jnp.bfloat16).astype(jnp.float32)


def mixer_kernel(
    rows, halo, packed_ref, cot_ref, short_ref, long_ref, skip_ref, mixed_ref, grad_ref,
    p0, p1, p2, cot, query, keyed, valued, gated, gradf,
):
    channels = SUB * LANES
    short_taps = short_ref.shape[0] // 3
    long_taps = long_ref.shape[0]
    spread = (p0, p1, p2)
    front = halo - long_taps

    @pl.loop(0, (rows + 2 * halo) // BLOCK)
    def _(i):
        at = pl.multiple_of(i * BLOCK, BLOCK)
        for g in range(3):
            for s in range(SUB):
                piece = packed_ref[pl.ds(at, BLOCK), pl.ds(g * channels + s * LANES, LANES)]
                spread[g][pl.ds(at * SUB + s, BLOCK, stride=SUB), :] = piece.astype(jnp.float32)

    @pl.loop(0, (rows + halo) // BLOCK)
    def _(i):
        at = pl.multiple_of(i * BLOCK, BLOCK)
        for s in range(SUB):
            piece = cot_ref[pl.ds(at, BLOCK), pl.ds(s * LANES, LANES)]
            cot[pl.ds(at * SUB + s, BLOCK, stride=SUB), :] = piece.astype(jnp.float32)

    def short(ref, g, first, sign):
        total = None
        for j in range(short_taps):
            term = short_ref[j * 3 + g][None] * tiles(ref, first + sign * j, SUB)
            total = term if total is None else total + term
        return total

    @pl.loop(0, (rows + BLOCK + long_taps) // SUB)
    def _(i):
        at = i * SUB
        key = short(p1, 1, at + front, -1)
        val = short(p2, 2, at + front, -1)
        put(keyed, at, key)
        put(valued, at, val)
        put(gated, at, rounded(key * val))

    @pl.loop(0, (rows + halo) // SUB)
    def _(i):
        at = i * SUB
        que = short(p0, 0, at + halo, -1)
        put(query, at, que)
        put(gradf, at, rounded(que * tiles(cot, at, SUB)))

    zero = tuple(jnp.zeros((SUB, LANES), jnp.float32) for _ in range(BLOCK))

    def long_sum(ref, base, sign):
        def chunk(c, acc):
            acc = list(acc)
            tap0 = c * CHUNK
            origin = base + sign * tap0
            low = origin - (CHUNK - 1) if sign < 0 else origin
            seen = {}

            def at(k):
                if k not in seen:
                    seen[k] = ref[pl.ds(pl.multiple_of((low + k) * SUB, SUB), SUB), :]
                return seen[k]

            for j in range(CHUNK):
                tap = long_ref[tap0 + j]
                for i in range(BLOCK):
                    k = i + (CHUNK - 1) - j if sign < 0 else i + j
                    acc[i] = acc[i] + tap * at(k)
            return tuple(acc)

        return lax.fori_loop(0, long_taps // CHUNK, chunk, zero)

    @pl.loop(0, (rows + BLOCK) // BLOCK)
    def _(b):
        at = b * BLOCK
        skip = skip_ref[...]
        ahead = jnp.stack(long_sum(gated, at + long_taps, -1))
        filtered = ahead + skip[None] * tiles(gated, at + long_taps, BLOCK)
        back = jnp.stack(long_sum(gradf, at, 1))
        grad_gated = back + skip[None] * tiles(gradf, at, BLOCK)
        put(p0, at, rounded(tiles(cot, at, BLOCK) * filtered))
        put(p1, at, rounded(grad_gated * tiles(valued, at + long_taps, BLOCK)))
        put(p2, at, rounded(grad_gated * tiles(keyed, at + long_taps, BLOCK)))
        put(gated, at, tiles(query, at, BLOCK) * filtered)

    results = (query, keyed, valued)

    @pl.loop(0, rows // SUB)
    def _(i):
        at = i * SUB
        for g in range(3):
            put(results[g], at, short(spread[g], g, at, 1))

    @pl.loop(0, rows // BLOCK)
    def _(i):
        at = pl.multiple_of(i * BLOCK, BLOCK)
        for s in range(SUB):
            pick = pl.ds(at * SUB + s, BLOCK, stride=SUB)
            mixed_ref[pl.ds(at, BLOCK), pl.ds(s * LANES, LANES)] = gated[pick, :].astype(jnp.bfloat16)
            for g in range(3):
                grad_ref[pl.ds(at, BLOCK), pl.ds(g * channels + s * LANES, LANES)] = results[g][
                    pick, :
                ].astype(jnp.bfloat16)


def mixer(packed, cot, short_filter, long_filter, skip_gain, rows, halo):
    channels = long_filter.shape[1]
    long_taps = long_filter.shape[0]
    full = (rows + 2 * halo) * SUB
    side = (rows + halo) * SUB
    scratch = [pltpu.VMEM((full, LANES), jnp.float32)] * 3 + [
        pltpu.VMEM((side, LANES), jnp.float32)
    ] * 6
    return pl.pallas_call(
        functools.partial(mixer_kernel, rows, halo),
        out_shape=(
            jax.ShapeDtypeStruct((rows, channels), jnp.bfloat16),
            jax.ShapeDtypeStruct((rows, 3 * channels), jnp.bfloat16),
        ),
        in_specs=[pl.BlockSpec(memory_space=pltpu.VMEM)] * 5,
        out_specs=(pl.BlockSpec(memory_space=pltpu.VMEM),) * 2,
        scratch_shapes=scratch,
        compiler_params=pltpu.CompilerParams(vmem_limit_bytes=52 << 20),
        cost_estimate=pl.CostEstimate(
            flops=4 * rows * channels * (long_taps + 42), bytes_accessed=12 << 20, transcendentals=0
        ),
    )(
        packed,
        cot,
        short_filter.reshape(-1, SUB, LANES),
        long_filter.reshape(long_taps, SUB, LANES),
        skip_gain.reshape(SUB, LANES),
    )


def finish_kernel(
    count, grad_ref, whole_ref, terms_ref, tokens_ref, sums_ref,
    held, total, mate, summed, ready, landed,
    send_one, recv_one, send_two, recv_two, send_tp, recv_tp, send_tok, recv_tok,
):
    me = lax.axis_index("ctx")
    mine = lax.axis_index("tp")
    other = 1 - mine
    width = mate.shape[1]
    cols = tokens_ref.shape[1]
    tile = ready.shape[2]
    steps = cols // tile

    barrier = pltpu.get_barrier_semaphore()
    for d in range(1, count):
        pl.semaphore_signal(
            barrier, inc=1, device_id={"ctx": lax.rem(me + d, count)}, device_id_type=pl.DeviceIdType.MESH
        )
    pl.semaphore_signal(barrier, inc=1, device_id={"tp": other}, device_id_type=pl.DeviceIdType.MESH)
    pl.semaphore_wait(barrier, count)

    first = []
    for d in range(1, count):
        peer = lax.rem(me + d, count)
        first.append(
            pltpu.make_async_remote_copy(
                src_ref=terms_ref.at[peer],
                dst_ref=held.at[d],
                send_sem=send_one.at[d],
                recv_sem=recv_one.at[d],
                device_id={"ctx": peer},
                device_id_type=pl.DeviceIdType.MESH,
            )
        )
        first[-1].start()

    def product(half, t):
        at = pl.multiple_of(half * cols + t * tile, tile)
        return lax.dot_general(
            grad_ref[...],
            whole_ref[pl.ds(at, tile), :],
            (((1,), (1,)), ((), ())),
            preferred_element_type=jnp.float32,
        )

    def token_copy(t):
        return pltpu.make_async_remote_copy(
            src_ref=ready.at[t],
            dst_ref=landed.at[t],
            send_sem=send_tok.at[t],
            recv_sem=recv_tok.at[t],
            device_id={"tp": other},
            device_id_type=pl.DeviceIdType.MESH,
        )

    @pl.loop(0, steps)
    def _(t):
        ready[t] = product(other, t).astype(jnp.bfloat16)
        token_copy(t).start()

    own = terms_ref[me]
    for d in range(1, count):
        first[d - 1].wait()
        own = own + held[d]
    total[...] = own
    tp_copy = pltpu.make_async_remote_copy(
        src_ref=total.at[:, pl.ds(0, width)],
        dst_ref=mate,
        send_sem=send_tp,
        recv_sem=recv_tp,
        device_id={"tp": other},
        device_id_type=pl.DeviceIdType.MESH,
    )
    tp_copy.start()

    def own_tile(t):
        value = product(mine, t)
        token_copy(t).wait()
        at = pl.multiple_of(t * tile, tile)
        tokens_ref[:, pl.ds(at, tile)] = (value + landed[t].astype(jnp.float32)).astype(jnp.bfloat16)

    pl.loop(0, steps // 4)(own_tile)
    tp_copy.wait()
    total[:, pl.ds(0, width)] = total[:, pl.ds(0, width)] + mate[...]
    summed[me] = total[...]
    second = []
    for d in range(1, count):
        second.append(
            pltpu.make_async_remote_copy(
                src_ref=total,
                dst_ref=summed.at[me],
                send_sem=send_two.at[d],
                recv_sem=recv_two.at[d],
                device_id={"ctx": lax.rem(me + d, count)},
                device_id_type=pl.DeviceIdType.MESH,
            )
        )
        second[-1].start()
    pl.loop(steps // 4, steps)(own_tile)
    for copy in second:
        copy.wait()
    sums_ref[...] = summed[...]


def finish(grad_packed, whole, part_a, part_b, count):
    rank, features = part_a.shape
    rows, wide = grad_packed.shape
    width, rest = features // count, wide // count
    cols = features // 2
    tile = 256
    terms = jnp.concatenate(
        [part_a.reshape(rank, count, width), part_b.reshape(rank, count, rest)], axis=2
    ).transpose(1, 0, 2)
    vmem = pl.BlockSpec(memory_space=pltpu.VMEM)
    grad_tokens, sums = pl.pallas_call(
        functools.partial(finish_kernel, count),
        out_shape=(
            jax.ShapeDtypeStruct((rows, cols), jnp.bfloat16),
            jax.ShapeDtypeStruct(terms.shape, jnp.float32),
        ),
        in_specs=[vmem] * 3,
        out_specs=(vmem, vmem),
        scratch_shapes=[
            pltpu.VMEM(terms.shape, jnp.float32),
            pltpu.VMEM((rank, width + rest), jnp.float32),
            pltpu.VMEM((rank, width), jnp.float32),
            pltpu.VMEM(terms.shape, jnp.float32),
            pltpu.VMEM((cols // tile, rows, tile), jnp.bfloat16),
            pltpu.VMEM((cols // tile, rows, tile), jnp.bfloat16),
            pltpu.SemaphoreType.DMA((count,)),
            pltpu.SemaphoreType.DMA((count,)),
            pltpu.SemaphoreType.DMA((count,)),
            pltpu.SemaphoreType.DMA((count,)),
            pltpu.SemaphoreType.DMA,
            pltpu.SemaphoreType.DMA,
            pltpu.SemaphoreType.DMA((cols // tile,)),
            pltpu.SemaphoreType.DMA((cols // tile,)),
        ],
        compiler_params=pltpu.CompilerParams(
            vmem_limit_bytes=48 << 20, collective_id=1, has_side_effects=True
        ),
        cost_estimate=pl.CostEstimate(
            flops=2 * rows * wide * features, bytes_accessed=20 << 20, transcendentals=0
        ),
    )(grad_packed, whole, terms)
    flat = sums.transpose(1, 0, 2)
    return (
        grad_tokens,
        flat[:, :, :width].reshape(rank, features),
        flat[:, :, width:].reshape(rank, wide),
    )


def body(tokens, weight, adapter_a, adapter_b, short_filter, long_filter, skip_gain, cotangent):
    row_count = tokens.shape[0]
    share_rows = weight.shape[0]
    channels = weight.shape[2]
    features = tokens.shape[1]
    adapter_rank = adapter_a.shape[1]
    halo = long_filter.shape[0] + BLOCK
    seq_total = row_count * lax.axis_size("ctx")
    first_row = lax.axis_index("ctx") * share_rows
    before = shifted(tokens[row_count - halo :], "ctx", 1)
    after = shifted(tokens[:halo], "ctx", -1)
    cot_after = shifted(cotangent[:halo], "ctx", -1)
    tokens_ext = jnp.concatenate([before, tokens, after], axis=0)
    cot_ext = jnp.concatenate([cotangent, cot_after], axis=0)
    own_rows = lax.dynamic_slice_in_dim(adapter_a, first_row, share_rows, 0)
    flat_b = adapter_b.reshape(adapter_rank, 3 * channels)
    delta_w = jnp.dot(own_rows, flat_b, preferred_element_type=jnp.float32)
    merged = (
        weight.reshape(share_rows, 3 * channels).astype(jnp.float32) + adapter_scale * delta_w
    ).astype(jnp.bfloat16)
    whole = lax.all_gather(merged, "ctx", axis=0, tiled=True)
    packed = jnp.dot(tokens_ext, whole, preferred_element_type=jnp.float32).astype(jnp.bfloat16)
    mixed, grad_packed = mixer(
        packed, cot_ext, short_filter, long_filter, skip_gain, row_count, halo
    )
    projected = jnp.dot(tokens, adapter_a, preferred_element_type=jnp.float32).astype(jnp.bfloat16)
    part_b = lax.dot_general(
        projected, grad_packed, (((0,), (0,)), ((), ())), preferred_element_type=jnp.float32
    )
    through = lax.dot_general(
        flat_b, grad_packed, (((1,), (1,)), ((), ())), preferred_element_type=jnp.float32
    ).astype(jnp.bfloat16)
    part_a = jnp.dot(through, tokens, preferred_element_type=jnp.float32)
    count = lax.axis_size("ctx")
    if features % (LANES * count) == 0 and (3 * channels) % (LANES * count) == 0:
        grad_tokens, sum_a, sum_b = finish(grad_packed, whole, part_a, part_b, count)
    else:
        sum_a = lax.psum(part_a, ("ctx", "tp"))
        sum_b = lax.psum(part_b, "ctx")
        partial_grad = lax.dot_general(
            grad_packed, whole, (((1,), (1,)), ((), ())), preferred_element_type=jnp.float32
        )
        grad_tokens = lax.psum_scatter(
            partial_grad.astype(jnp.bfloat16), "tp", scatter_dimension=1, tiled=True
        )
    sum_a = sum_a.T
    factor = adapter_scale / math.sqrt(seq_total)
    return (mixed, grad_tokens, sum_a * factor, (sum_b * factor).reshape(adapter_rank, 3, channels))


def solution(mesh):
    return jax.shard_map(
        body,
        mesh=mesh,
        in_specs=(
            P(("groups", "ctx"), None),
            P("ctx", None, "tp"),
            P(),
            P(None, None, "tp"),
            P(None, None, "tp"),
            P(None, "tp"),
            P("tp"),
            P(("groups", "ctx"), "tp"),
        ),
        out_specs=(
            P(("groups", "ctx"), "tp"),
            P(("groups", "ctx"), "tp"),
            P("groups", None),
            P("groups", None, "tp"),
        ),
        check_vma=False,
    )
```

```python
import functools
import math

import jax
import jax.numpy as jnp
from jax import lax
from jax.experimental import pallas as pl
from jax.experimental.pallas import tpu as pltpu
from jax.sharding import PartitionSpec as P

adapter_scale = 0.03125
LANES = 128
SUB = 8
BLOCK = 16
CHUNK = 32


def shifted(value, axis, steps):
    count = lax.axis_size(axis)
    initial, last = (max(0, -steps), min(count, count - steps))
    return lax.ppermute(value, axis, [(source, source + steps) for source in range(initial, last)])


def tiles(ref, first, count):
    start = first * SUB
    if not isinstance(start, int):
        start = pl.multiple_of(start, SUB)
    return ref[pl.ds(start, count * SUB), :].reshape(count, SUB, LANES)


def put(ref, first, value):
    count = value.shape[0]
    ref[pl.ds(pl.multiple_of(first * SUB, SUB), count * SUB), :] = value.reshape(count * SUB, LANES)


def rounded(value):
    return value.astype(jnp.bfloat16).astype(jnp.float32)


def mixer_kernel(
    rows, halo, packed_ref, cot_ref, short_ref, long_ref, skip_ref, mixed_ref, grad_ref,
    p0, p1, p2, cot, query, keyed, valued, gated, gradf,
):
    channels = SUB * LANES
    short_taps = short_ref.shape[0] // 3
    long_taps = long_ref.shape[0]
    spread = (p0, p1, p2)
    front = halo - long_taps

    @pl.loop(0, (rows + 2 * halo) // BLOCK)
    def _(i):
        at = pl.multiple_of(i * BLOCK, BLOCK)
        for g in range(3):
            for s in range(SUB):
                piece = packed_ref[pl.ds(at, BLOCK), pl.ds(g * channels + s * LANES, LANES)]
                spread[g][pl.ds(at * SUB + s, BLOCK, stride=SUB), :] = piece.astype(jnp.float32)

    @pl.loop(0, (rows + halo) // BLOCK)
    def _(i):
        at = pl.multiple_of(i * BLOCK, BLOCK)
        for s in range(SUB):
            piece = cot_ref[pl.ds(at, BLOCK), pl.ds(s * LANES, LANES)]
            cot[pl.ds(at * SUB + s, BLOCK, stride=SUB), :] = piece.astype(jnp.float32)

    def short(ref, g, first, sign):
        total = None
        for j in range(short_taps):
            term = short_ref[j * 3 + g][None] * tiles(ref, first + sign * j, SUB)
            total = term if total is None else total + term
        return total

    @pl.loop(0, (rows + BLOCK + long_taps) // SUB)
    def _(i):
        at = i * SUB
        key = short(p1, 1, at + front, -1)
        val = short(p2, 2, at + front, -1)
        put(keyed, at, key)
        put(valued, at, val)
        put(gated, at, rounded(key * val))

    @pl.loop(0, (rows + halo) // SUB)
    def _(i):
        at = i * SUB
        que = short(p0, 0, at + halo, -1)
        put(query, at, que)
        put(gradf, at, rounded(que * tiles(cot, at, SUB)))

    zero = tuple(jnp.zeros((SUB, LANES), jnp.float32) for _ in range(BLOCK))

    def long_sum(ref, base, sign):
        def chunk(c, acc):
            acc = list(acc)
            tap0 = c * CHUNK
            origin = base + sign * tap0
            low = origin - (CHUNK - 1) if sign < 0 else origin
            seen = {}

            def at(k):
                if k not in seen:
                    seen[k] = ref[pl.ds(pl.multiple_of((low + k) * SUB, SUB), SUB), :]
                return seen[k]

            for j in range(CHUNK):
                tap = long_ref[tap0 + j]
                for i in range(BLOCK):
                    k = i + (CHUNK - 1) - j if sign < 0 else i + j
                    acc[i] = acc[i] + tap * at(k)
            return tuple(acc)

        return lax.fori_loop(0, long_taps // CHUNK, chunk, zero)

    @pl.loop(0, (rows + BLOCK) // BLOCK)
    def _(b):
        at = b * BLOCK
        skip = skip_ref[...]
        ahead = jnp.stack(long_sum(gated, at + long_taps, -1))
        filtered = ahead + skip[None] * tiles(gated, at + long_taps, BLOCK)
        back = jnp.stack(long_sum(gradf, at, 1))
        grad_gated = back + skip[None] * tiles(gradf, at, BLOCK)
        put(p0, at, rounded(tiles(cot, at, BLOCK) * filtered))
        put(p1, at, rounded(grad_gated * tiles(valued, at + long_taps, BLOCK)))
        put(p2, at, rounded(grad_gated * tiles(keyed, at + long_taps, BLOCK)))
        put(gated, at, tiles(query, at, BLOCK) * filtered)

    results = (query, keyed, valued)

    @pl.loop(0, rows // SUB)
    def _(i):
        at = i * SUB
        for g in range(3):
            put(results[g], at, short(spread[g], g, at, 1))

    @pl.loop(0, rows // BLOCK)
    def _(i):
        at = pl.multiple_of(i * BLOCK, BLOCK)
        for s in range(SUB):
            pick = pl.ds(at * SUB + s, BLOCK, stride=SUB)
            mixed_ref[pl.ds(at, BLOCK), pl.ds(s * LANES, LANES)] = gated[pick, :].astype(jnp.bfloat16)
            for g in range(3):
                grad_ref[pl.ds(at, BLOCK), pl.ds(g * channels + s * LANES, LANES)] = results[g][
                    pick, :
                ].astype(jnp.bfloat16)


def mixer(packed, cot, short_filter, long_filter, skip_gain, rows, halo):
    channels = long_filter.shape[1]
    long_taps = long_filter.shape[0]
    full = (rows + 2 * halo) * SUB
    side = (rows + halo) * SUB
    scratch = [pltpu.VMEM((full, LANES), jnp.float32)] * 3 + [
        pltpu.VMEM((side, LANES), jnp.float32)
    ] * 6
    return pl.pallas_call(
        functools.partial(mixer_kernel, rows, halo),
        out_shape=(
            jax.ShapeDtypeStruct((rows, channels), jnp.bfloat16),
            jax.ShapeDtypeStruct((rows, 3 * channels), jnp.bfloat16),
        ),
        in_specs=[pl.BlockSpec(memory_space=pltpu.VMEM)] * 5,
        out_specs=(pl.BlockSpec(memory_space=pltpu.VMEM),) * 2,
        scratch_shapes=scratch,
        compiler_params=pltpu.CompilerParams(vmem_limit_bytes=52 << 20),
        cost_estimate=pl.CostEstimate(
            flops=4 * rows * channels * (long_taps + 42), bytes_accessed=12 << 20, transcendentals=0
        ),
    )(
        packed,
        cot,
        short_filter.reshape(-1, SUB, LANES),
        long_filter.reshape(long_taps, SUB, LANES),
        skip_gain.reshape(SUB, LANES),
    )


def finish_kernel(
    count, grad_ref, whole_ref, terms_ref, tokens_ref, sums_ref,
    held, total, mate, summed, ready, landed,
    send_one, recv_one, send_two, recv_two, send_tp, recv_tp, send_tok, recv_tok,
):
    me = lax.axis_index("ctx")
    mine = lax.axis_index("tp")
    other = 1 - mine
    width = mate.shape[1]
    cols = tokens_ref.shape[1]
    tile = ready.shape[2]
    steps = cols // tile

    barrier = pltpu.get_barrier_semaphore()
    for d in range(1, count):
        pl.semaphore_signal(
            barrier, inc=1, device_id={"ctx": lax.rem(me + d, count)}, device_id_type=pl.DeviceIdType.MESH
        )
    pl.semaphore_signal(barrier, inc=1, device_id={"tp": other}, device_id_type=pl.DeviceIdType.MESH)
    pl.semaphore_wait(barrier, count)

    first = []
    for d in range(1, count):
        peer = lax.rem(me + d, count)
        first.append(
            pltpu.make_async_remote_copy(
                src_ref=terms_ref.at[peer],
                dst_ref=held.at[d],
                send_sem=send_one.at[d],
                recv_sem=recv_one.at[d],
                device_id={"ctx": peer},
                device_id_type=pl.DeviceIdType.MESH,
            )
        )
        first[-1].start()

    def product(half, t):
        at = pl.multiple_of(half * cols + t * tile, tile)
        return lax.dot_general(
            grad_ref[...],
            whole_ref[pl.ds(at, tile), :],
            (((1,), (1,)), ((), ())),
            preferred_element_type=jnp.float32,
        )

    def token_copy(t):
        return pltpu.make_async_remote_copy(
            src_ref=ready.at[t],
            dst_ref=landed.at[t],
            send_sem=send_tok.at[t],
            recv_sem=recv_tok.at[t],
            device_id={"tp": other},
            device_id_type=pl.DeviceIdType.MESH,
        )

    @pl.loop(0, steps)
    def _(t):
        ready[t] = product(other, t).astype(jnp.bfloat16)
        token_copy(t).start()

    own = terms_ref[me]
    for d in range(1, count):
        first[d - 1].wait()
        own = own + held[d]
    total[...] = own
    tp_copy = pltpu.make_async_remote_copy(
        src_ref=total.at[:, pl.ds(0, width)],
        dst_ref=mate,
        send_sem=send_tp,
        recv_sem=recv_tp,
        device_id={"tp": other},
        device_id_type=pl.DeviceIdType.MESH,
    )
    tp_copy.start()

    def own_tile(t):
        value = product(mine, t)
        token_copy(t).wait()
        at = pl.multiple_of(t * tile, tile)
        tokens_ref[:, pl.ds(at, tile)] = (value + landed[t].astype(jnp.float32)).astype(jnp.bfloat16)

    pl.loop(0, steps // 4)(own_tile)
    tp_copy.wait()
    total[:, pl.ds(0, width)] = total[:, pl.ds(0, width)] + mate[...]
    summed[me] = total[...]
    second = []
    for d in range(1, count):
        second.append(
            pltpu.make_async_remote_copy(
                src_ref=total,
                dst_ref=summed.at[me],
                send_sem=send_two.at[d],
                recv_sem=recv_two.at[d],
                device_id={"ctx": lax.rem(me + d, count)},
                device_id_type=pl.DeviceIdType.MESH,
            )
        )
        second[-1].start()
    pl.loop(steps // 4, steps)(own_tile)
    for copy in second:
        copy.wait()
    sums_ref[...] = summed[...]


def finish(grad_packed, whole, part_a, part_b, count):
    rank, features = part_a.shape
    rows, wide = grad_packed.shape
    width, rest = features // count, wide // count
    cols = features // 2
    tile = 256
    terms = jnp.concatenate(
        [part_a.reshape(rank, count, width), part_b.reshape(rank, count, rest)], axis=2
    ).transpose(1, 0, 2)
    vmem = pl.BlockSpec(memory_space=pltpu.VMEM)
    grad_tokens, sums = pl.pallas_call(
        functools.partial(finish_kernel, count),
        out_shape=(
            jax.ShapeDtypeStruct((rows, cols), jnp.bfloat16),
            jax.ShapeDtypeStruct(terms.shape, jnp.float32),
        ),
        in_specs=[vmem] * 3,
        out_specs=(vmem, vmem),
        scratch_shapes=[
            pltpu.VMEM(terms.shape, jnp.float32),
            pltpu.VMEM((rank, width + rest), jnp.float32),
            pltpu.VMEM((rank, width), jnp.float32),
            pltpu.VMEM(terms.shape, jnp.float32),
            pltpu.VMEM((cols // tile, rows, tile), jnp.bfloat16),
            pltpu.VMEM((cols // tile, rows, tile), jnp.bfloat16),
            pltpu.SemaphoreType.DMA((count,)),
            pltpu.SemaphoreType.DMA((count,)),
            pltpu.SemaphoreType.DMA((count,)),
            pltpu.SemaphoreType.DMA((count,)),
            pltpu.SemaphoreType.DMA,
            pltpu.SemaphoreType.DMA,
            pltpu.SemaphoreType.DMA((cols // tile,)),
            pltpu.SemaphoreType.DMA((cols // tile,)),
        ],
        compiler_params=pltpu.CompilerParams(
            vmem_limit_bytes=48 << 20, collective_id=1, has_side_effects=True
        ),
        cost_estimate=pl.CostEstimate(
            flops=2 * rows * wide * features, bytes_accessed=20 << 20, transcendentals=0
        ),
    )(grad_packed, whole, terms)
    flat = sums.transpose(1, 0, 2)
    return (
        grad_tokens,
        flat[:, :, :width].reshape(rank, features),
        flat[:, :, width:].reshape(rank, wide),
    )


MESH = pl.DeviceIdType.MESH
PIECES = 4


def gather_kernel(
    outer, shard_ref, out_ref, z_send, z_recv, y_send, y_recv, x_send, x_recv, local_sem
):
    me = lax.axis_index("ctx")
    x = lax.axis_index("groups")
    z, y = me // 2, lax.rem(me, 2)
    rows = shard_ref.shape[0]
    piece = rows // PIECES
    half = piece // 2
    last = outer - 2
    steps = outer - 1

    def ctx_of(line, pair):
        return {"ctx": line * 2 + pair}

    def span(line, pair, start, size):
        return pl.ds(pl.multiple_of((line * 2 + pair) * rows + start, half), size)

    def part(p, side):
        return p * piece + side * half

    def copy(src, dst, send, recv, device):
        return pltpu.make_async_remote_copy(
            src_ref=src, dst_ref=dst, send_sem=send, recv_sem=recv, device_id=device, device_id_type=MESH
        )

    def z_range(k, p):
        return (part(p, x), half) if k == last else (p * piece, piece)

    def z_out(way, k, p):
        step = 1 - 2 * way
        start, size = z_range(k, p)
        place = span(z - step * k, y, start, size)
        src = out_ref.at[place] if k else shard_ref.at[pl.ds(pl.multiple_of(start, half), size)]
        return copy(
            src, out_ref.at[place], z_send.at[way, k, p], z_recv.at[way, k, p], ctx_of(z + step, y)
        )

    def z_in(way, k, p):
        step = 1 - 2 * way
        start, size = z_range(k, p)
        place = out_ref.at[span(z - step * (k + 1), y, start, size)]
        return copy(place, place, z_send.at[way, k, p], z_recv.at[way, k, p], ctx_of(z - step, y))

    def sends(way, k):
        return (z < steps) & (z >= k) if way == 0 else (z > 0) & (z + k <= steps)

    def receives(way, k):
        return z > k if way == 0 else z + k < steps

    def line_of(i):
        if i == 0:
            return z
        way, k = (i - 1) // steps, (i - 1) % steps
        return z - (1 - 2 * way) * (k + 1)

    def item(way, k):
        return 1 + way * steps + k

    def y_out(i, p):
        start = part(p, x)
        place = span(line_of(i), y, start, half)
        src = out_ref.at[place] if i else shard_ref.at[pl.ds(pl.multiple_of(start, half), half)]
        return copy(src, out_ref.at[place], y_send.at[i, p], y_recv.at[i, p], ctx_of(z, 1 - y))

    def y_in(i, p):
        place = out_ref.at[span(line_of(i), 1 - y, part(p, x), half)]
        return copy(place, place, y_send.at[i, p], y_recv.at[i, p], ctx_of(z, 1 - y))

    def x_copy(i, p, side):
        if i > 2 * steps:
            line, pair = line_of(item(i - 2 * steps - 1, last)), y
        else:
            line, pair = line_of(i), 1 - y
        place = out_ref.at[span(line, pair, part(p, side), half)]
        return copy(place, place, x_send.at[i, p], x_recv.at[i, p], {"groups": 1 - x})

    def extra(way):
        return 2 * steps + 1 + way

    barrier = pltpu.get_barrier_semaphore()
    pl.semaphore_signal(barrier, inc=1, device_id=ctx_of(z, 1 - y), device_id_type=MESH)
    pl.semaphore_signal(barrier, inc=1, device_id={"groups": 1 - x}, device_id_type=MESH)
    for step in (1, outer - 1):
        pl.semaphore_signal(
            barrier, inc=1, device_id=ctx_of(lax.rem(z + step, outer), y), device_id_type=MESH
        )
    pl.semaphore_wait(barrier, 4)

    @pl.loop(0, PIECES)
    def _(p):
        for way in range(2):
            @pl.when(sends(way, 0))
            def _():
                z_out(way, 0, p).start()
        y_out(0, p).start()

    own = pltpu.make_async_copy(
        shard_ref, out_ref.at[pl.ds(pl.multiple_of(me * rows, rows), rows)], local_sem
    )
    own.start()

    def pass_on(k, p):
        for way in range(2):
            @pl.when(receives(way, k))
            def _():
                i = item(way, k)
                y_in(i, p).wait_recv()
                x_copy(i, p, x).start()

    for k in range(steps):
        @pl.loop(0, PIECES)
        def _(p):
            for way in range(2):
                @pl.when(receives(way, k))
                def _():
                    z_in(way, k, p).wait_recv()
                    if k < last:
                        @pl.when(sends(way, k + 1))
                        def _():
                            z_out(way, k + 1, p).start()
                    y_out(item(way, k), p).start()
                    if k == last:
                        x_copy(extra(way), p, x).start()
            if k == 0:
                y_in(0, p).wait_recv()
                x_copy(0, p, x).start()

            @pl.when(p > 0)
            def _():
                pass_on(k, p - 1)

            if k > 0:
                @pl.when(p == 0)
                def _():
                    pass_on(k - 1, PIECES - 1)

    pass_on(last, PIECES - 1)
    own.wait()

    @pl.loop(0, PIECES)
    def _(p):
        x_copy(0, p, 1 - x).wait_recv()
        x_copy(0, p, x).wait_send()
        y_out(0, p).wait_send()
        for way in range(2):
            for k in range(steps):
                @pl.when(sends(way, k))
                def _():
                    z_out(way, k, p).wait_send()

                @pl.when(receives(way, k))
                def _():
                    i = item(way, k)
                    x_copy(i, p, 1 - x).wait_recv()
                    x_copy(i, p, x).wait_send()
                    y_out(i, p).wait_send()
                    if k == last:
                        x_copy(extra(way), p, 1 - x).wait_recv()
                        x_copy(extra(way), p, x).wait_send()


def gather(merged, count):
    rows, wide = merged.shape
    outer = count // 2
    items = 2 * (outer - 1) + 1
    dma = pltpu.SemaphoreType.DMA
    hbm = pl.BlockSpec(memory_space=pl.ANY)
    return pl.pallas_call(
        functools.partial(gather_kernel, outer),
        out_shape=jax.ShapeDtypeStruct((rows * count, wide), merged.dtype),
        in_specs=[hbm],
        out_specs=hbm,
        scratch_shapes=[
            dma((2, outer - 1, PIECES)),
            dma((2, outer - 1, PIECES)),
            dma((items, PIECES)),
            dma((items, PIECES)),
            dma((items + 2, PIECES)),
            dma((items + 2, PIECES)),
            dma,
        ],
        compiler_params=pltpu.CompilerParams(collective_id=2, has_side_effects=True),
        cost_estimate=pl.CostEstimate(flops=0, bytes_accessed=300 << 20, transcendentals=0),
    )(merged)


def body(tokens, weight, adapter_a, adapter_b, short_filter, long_filter, skip_gain, cotangent):
    row_count = tokens.shape[0]
    share_rows = weight.shape[0]
    channels = weight.shape[2]
    features = tokens.shape[1]
    adapter_rank = adapter_a.shape[1]
    halo = long_filter.shape[0] + BLOCK
    count = lax.axis_size("ctx")
    seq_total = row_count * count
    first_row = lax.axis_index("ctx") * share_rows
    before = shifted(tokens[row_count - halo :], "ctx", 1)
    after = shifted(tokens[:halo], "ctx", -1)
    cot_after = shifted(cotangent[:halo], "ctx", -1)
    tokens_ext = jnp.concatenate([before, tokens, after], axis=0)
    cot_ext = jnp.concatenate([cotangent, cot_after], axis=0)
    own_rows = lax.dynamic_slice_in_dim(adapter_a, first_row, share_rows, 0)
    flat_b = adapter_b.reshape(adapter_rank, 3 * channels)
    delta_w = jnp.dot(own_rows, flat_b, preferred_element_type=jnp.float32)
    merged = (
        weight.reshape(share_rows, 3 * channels).astype(jnp.float32) + adapter_scale * delta_w
    ).astype(jnp.bfloat16)
    if count == 8 and lax.axis_size("groups") == 2:
        whole = gather(merged, count)
    else:
        whole = lax.all_gather(merged, "ctx", axis=0, tiled=True)
    packed = jnp.dot(tokens_ext, whole, preferred_element_type=jnp.float32).astype(jnp.bfloat16)
    mixed, grad_packed = mixer(
        packed, cot_ext, short_filter, long_filter, skip_gain, row_count, halo
    )
    projected = jnp.dot(tokens, adapter_a, preferred_element_type=jnp.float32).astype(jnp.bfloat16)
    part_b = lax.dot_general(
        projected, grad_packed, (((0,), (0,)), ((), ())), preferred_element_type=jnp.float32
    )
    through = lax.dot_general(
        flat_b, grad_packed, (((1,), (1,)), ((), ())), preferred_element_type=jnp.float32
    ).astype(jnp.bfloat16)
    part_a = jnp.dot(through, tokens, preferred_element_type=jnp.float32)
    if features % (LANES * count) == 0 and (3 * channels) % (LANES * count) == 0:
        grad_tokens, sum_a, sum_b = finish(grad_packed, whole, part_a, part_b, count)
    else:
        sum_a = lax.psum(part_a, ("ctx", "tp"))
        sum_b = lax.psum(part_b, "ctx")
        partial_grad = lax.dot_general(
            grad_packed, whole, (((1,), (1,)), ((), ())), preferred_element_type=jnp.float32
        )
        grad_tokens = lax.psum_scatter(
            partial_grad.astype(jnp.bfloat16), "tp", scatter_dimension=1, tiled=True
        )
    sum_a = sum_a.T
    factor = adapter_scale / math.sqrt(seq_total)
    return (mixed, grad_tokens, sum_a * factor, (sum_b * factor).reshape(adapter_rank, 3, channels))


def solution(mesh):
    return jax.shard_map(
        body,
        mesh=mesh,
        in_specs=(
            P(("groups", "ctx"), None),
            P("ctx", None, "tp"),
            P(),
            P(None, None, "tp"),
            P(None, None, "tp"),
            P(None, "tp"),
            P("tp"),
            P(("groups", "ctx"), "tp"),
        ),
        out_specs=(
            P(("groups", "ctx"), "tp"),
            P(("groups", "ctx"), "tp"),
            P("groups", None),
            P("groups", None, "tp"),
        ),
        check_vma=False,
    )
```

```python
import functools
import math

import jax
import jax.numpy as jnp
from jax import lax
from jax.experimental import pallas as pl
from jax.experimental.pallas import tpu as pltpu
from jax.sharding import PartitionSpec as P

adapter_scale = 0.03125
LANES = 128
SUB = 8
BLOCK = 16
CHUNK = 32
GROUP = 8


def shifted(value, axis, steps):
    count = lax.axis_size(axis)
    initial, last = (max(0, -steps), min(count, count - steps))
    return lax.ppermute(value, axis, [(source, source + steps) for source in range(initial, last)])


def tiles(ref, first, count):
    start = first * SUB
    if not isinstance(start, int):
        start = pl.multiple_of(start, SUB)
    return ref[pl.ds(start, count * SUB), :].reshape(count, SUB, LANES)


def put(ref, first, value):
    count = value.shape[0]
    ref[pl.ds(pl.multiple_of(first * SUB, SUB), count * SUB), :] = value.reshape(count * SUB, LANES)


def rounded(value):
    return value.astype(jnp.bfloat16).astype(jnp.float32)


def mixer_kernel(
    rows, halo, packed_ref, cot_ref, short_ref, long_ref, skip_ref, mixed_ref, grad_ref,
    p0, p1, p2, cot, query, keyed, valued, gated, gradf, gated_two, gradf_two,
):
    channels = SUB * LANES
    short_taps = short_ref.shape[0] // 3
    long_taps = long_ref.shape[0]
    spread = (p0, p1, p2)
    front = halo - long_taps

    @pl.loop(0, (rows + 2 * halo) // BLOCK)
    def _(i):
        at = pl.multiple_of(i * BLOCK, BLOCK)
        for g in range(3):
            for s in range(SUB):
                piece = packed_ref[pl.ds(at, BLOCK), pl.ds(g * channels + s * LANES, LANES)]
                spread[g][pl.ds(at * SUB + s, BLOCK, stride=SUB), :] = piece.astype(jnp.float32)

    @pl.loop(0, (rows + halo) // BLOCK)
    def _(i):
        at = pl.multiple_of(i * BLOCK, BLOCK)
        for s in range(SUB):
            piece = cot_ref[pl.ds(at, BLOCK), pl.ds(s * LANES, LANES)]
            cot[pl.ds(at * SUB + s, BLOCK, stride=SUB), :] = piece.astype(jnp.float32)

    def short(ref, g, first, sign):
        total = None
        for j in range(short_taps):
            term = short_ref[j * 3 + g][None] * tiles(ref, first + sign * j, SUB)
            total = term if total is None else total + term
        return total

    @pl.loop(0, (rows + BLOCK + long_taps) // SUB)
    def _(i):
        at = i * SUB
        key = short(p1, 1, at + front, -1)
        val = short(p2, 2, at + front, -1)
        put(keyed, at, key)
        put(valued, at, val)
        put(gated, at, rounded(key * val))

    @pl.loop(0, (rows + halo) // SUB)
    def _(i):
        at = i * SUB
        que = short(p0, 0, at + halo, -1)
        put(query, at, que)
        put(gradf, at, rounded(que * tiles(cot, at, SUB)))

    apart = (rows + BLOCK) // 2

    @pl.loop(0, (apart + long_taps) // SUB)
    def _(i):
        at = i * SUB
        for source, target in ((gated, gated_two), (gradf, gradf_two)):
            both = jnp.concatenate([tiles(source, at, SUB), tiles(source, at + apart, SUB)], axis=1)
            target[pl.ds(at, SUB)] = both.astype(jnp.bfloat16)

    zero = tuple(jnp.zeros((2 * SUB, LANES), jnp.float32) for _ in range(SUB))

    def long_sum(ref, base, sign):
        def chunk(c, acc):
            acc = list(acc)
            tap0 = c * CHUNK
            origin = base + sign * tap0
            low = origin - (CHUNK - 1) if sign < 0 else origin
            seen = {}

            def at(k):
                if k not in seen:
                    seen[k] = ref[low + k]
                return seen[k]

            for group in range(CHUNK // GROUP):
                taps = [long_ref[tap0 + group * GROUP + j] for j in range(GROUP)]
                for i in range(SUB):
                    terms = []
                    for j in range(GROUP):
                        tap = group * GROUP + j
                        k = i + (CHUNK - 1) - tap if sign < 0 else i + tap
                        terms.append(taps[j] * at(k))
                    while len(terms) > 1:
                        terms = [terms[n] + terms[n + 1] for n in range(0, len(terms), 2)]
                    acc[i] = acc[i] + terms[0].astype(jnp.float32)
            return tuple(acc)

        return lax.fori_loop(0, long_taps // CHUNK, chunk, zero)

    @pl.loop(0, apart // SUB)
    def _(b):
        skip = skip_ref[...]
        ahead = jnp.stack(long_sum(gated_two, b * SUB + long_taps, -1))
        back = jnp.stack(long_sum(gradf_two, b * SUB, 1))
        for side in range(2):
            at = b * SUB + side * apart
            pick = slice(side * SUB, (side + 1) * SUB)
            filtered = ahead[:, pick] + skip[None] * tiles(gated, at + long_taps, SUB)
            grad_gated = back[:, pick] + skip[None] * tiles(gradf, at, SUB)
            put(p0, at, rounded(tiles(cot, at, SUB) * filtered))
            put(p1, at, rounded(grad_gated * tiles(valued, at + long_taps, SUB)))
            put(p2, at, rounded(grad_gated * tiles(keyed, at + long_taps, SUB)))
            put(cot, at, tiles(query, at, SUB) * filtered)

    results = (query, keyed, valued)

    @pl.loop(0, rows // SUB)
    def _(i):
        at = i * SUB
        for g in range(3):
            put(results[g], at, short(spread[g], g, at, 1))

    @pl.loop(0, rows // BLOCK)
    def _(i):
        at = pl.multiple_of(i * BLOCK, BLOCK)
        for s in range(SUB):
            pick = pl.ds(at * SUB + s, BLOCK, stride=SUB)
            mixed_ref[pl.ds(at, BLOCK), pl.ds(s * LANES, LANES)] = cot[pick, :].astype(jnp.bfloat16)
            for g in range(3):
                grad_ref[pl.ds(at, BLOCK), pl.ds(g * channels + s * LANES, LANES)] = results[g][
                    pick, :
                ].astype(jnp.bfloat16)


def mixer(packed, cot, short_filter, long_filter, skip_gain, rows, halo):
    channels = long_filter.shape[1]
    long_taps = long_filter.shape[0]
    full = (rows + 2 * halo) * SUB
    side = (rows + halo) * SUB
    scratch = [pltpu.VMEM((full, LANES), jnp.float32)] * 3 + [
        pltpu.VMEM((side, LANES), jnp.float32)
    ] * 6
    pairs = ((rows + BLOCK) // 2 + long_taps, 2 * SUB, LANES)
    scratch += [pltpu.VMEM(pairs, jnp.bfloat16)] * 2
    taps = long_filter.reshape(long_taps, SUB, LANES).astype(jnp.bfloat16)
    return pl.pallas_call(
        functools.partial(mixer_kernel, rows, halo),
        out_shape=(
            jax.ShapeDtypeStruct((rows, channels), jnp.bfloat16),
            jax.ShapeDtypeStruct((rows, 3 * channels), jnp.bfloat16),
        ),
        in_specs=[pl.BlockSpec(memory_space=pltpu.VMEM)] * 5,
        out_specs=(pl.BlockSpec(memory_space=pltpu.VMEM),) * 2,
        scratch_shapes=scratch,
        compiler_params=pltpu.CompilerParams(vmem_limit_bytes=52 << 20),
        cost_estimate=pl.CostEstimate(
            flops=4 * rows * channels * (long_taps + 42), bytes_accessed=12 << 20, transcendentals=0
        ),
    )(
        packed,
        cot,
        short_filter.reshape(-1, SUB, LANES),
        jnp.concatenate([taps, taps], axis=1),
        skip_gain.reshape(SUB, LANES),
    )


def finish_kernel(
    count, grad_ref, whole_ref, terms_ref, tokens_ref, sums_ref,
    held, total, mate, summed, ready, landed,
    send_one, recv_one, send_two, recv_two, send_tp, recv_tp, send_tok, recv_tok,
):
    me = lax.axis_index("ctx")
    mine = lax.axis_index("tp")
    other = 1 - mine
    width = mate.shape[1]
    cols = tokens_ref.shape[1]
    tile = ready.shape[2]
    steps = cols // tile

    barrier = pltpu.get_barrier_semaphore()
    for d in range(1, count):
        pl.semaphore_signal(
            barrier, inc=1, device_id={"ctx": lax.rem(me + d, count)}, device_id_type=pl.DeviceIdType.MESH
        )
    pl.semaphore_signal(barrier, inc=1, device_id={"tp": other}, device_id_type=pl.DeviceIdType.MESH)
    pl.semaphore_wait(barrier, count)

    first = []
    for d in range(1, count):
        peer = lax.rem(me + d, count)
        first.append(
            pltpu.make_async_remote_copy(
                src_ref=terms_ref.at[peer],
                dst_ref=held.at[d],
                send_sem=send_one.at[d],
                recv_sem=recv_one.at[d],
                device_id={"ctx": peer},
                device_id_type=pl.DeviceIdType.MESH,
            )
        )
        first[-1].start()

    def product(half, t):
        at = pl.multiple_of(half * cols + t * tile, tile)
        return lax.dot_general(
            grad_ref[...],
            whole_ref[pl.ds(at, tile), :],
            (((1,), (1,)), ((), ())),
            preferred_element_type=jnp.float32,
        )

    def token_copy(t):
        return pltpu.make_async_remote_copy(
            src_ref=ready.at[t],
            dst_ref=landed.at[t],
            send_sem=send_tok.at[t],
            recv_sem=recv_tok.at[t],
            device_id={"tp": other},
            device_id_type=pl.DeviceIdType.MESH,
        )

    @pl.loop(0, steps)
    def _(t):
        ready[t] = product(other, t).astype(jnp.bfloat16)
        token_copy(t).start()

    own = terms_ref[me]
    for d in range(1, count):
        first[d - 1].wait()
        own = own + held[d]
    total[...] = own
    tp_copy = pltpu.make_async_remote_copy(
        src_ref=total.at[:, pl.ds(0, width)],
        dst_ref=mate,
        send_sem=send_tp,
        recv_sem=recv_tp,
        device_id={"tp": other},
        device_id_type=pl.DeviceIdType.MESH,
    )
    tp_copy.start()

    def own_tile(t):
        value = product(mine, t)
        token_copy(t).wait()
        at = pl.multiple_of(t * tile, tile)
        tokens_ref[:, pl.ds(at, tile)] = (value + landed[t].astype(jnp.float32)).astype(jnp.bfloat16)

    pl.loop(0, steps // 4)(own_tile)
    tp_copy.wait()
    total[:, pl.ds(0, width)] = total[:, pl.ds(0, width)] + mate[...]
    summed[me] = total[...]
    second = []
    for d in range(1, count):
        second.append(
            pltpu.make_async_remote_copy(
                src_ref=total,
                dst_ref=summed.at[me],
                send_sem=send_two.at[d],
                recv_sem=recv_two.at[d],
                device_id={"ctx": lax.rem(me + d, count)},
                device_id_type=pl.DeviceIdType.MESH,
            )
        )
        second[-1].start()
    pl.loop(steps // 4, steps)(own_tile)
    for copy in second:
        copy.wait()
    sums_ref[...] = summed[...]


def finish(grad_packed, whole, part_a, part_b, count):
    rank, features = part_a.shape
    rows, wide = grad_packed.shape
    width, rest = features // count, wide // count
    cols = features // 2
    tile = 256
    terms = jnp.concatenate(
        [part_a.reshape(rank, count, width), part_b.reshape(rank, count, rest)], axis=2
    ).transpose(1, 0, 2)
    vmem = pl.BlockSpec(memory_space=pltpu.VMEM)
    grad_tokens, sums = pl.pallas_call(
        functools.partial(finish_kernel, count),
        out_shape=(
            jax.ShapeDtypeStruct((rows, cols), jnp.bfloat16),
            jax.ShapeDtypeStruct(terms.shape, jnp.float32),
        ),
        in_specs=[vmem] * 3,
        out_specs=(vmem, vmem),
        scratch_shapes=[
            pltpu.VMEM(terms.shape, jnp.float32),
            pltpu.VMEM((rank, width + rest), jnp.float32),
            pltpu.VMEM((rank, width), jnp.float32),
            pltpu.VMEM(terms.shape, jnp.float32),
            pltpu.VMEM((cols // tile, rows, tile), jnp.bfloat16),
            pltpu.VMEM((cols // tile, rows, tile), jnp.bfloat16),
            pltpu.SemaphoreType.DMA((count,)),
            pltpu.SemaphoreType.DMA((count,)),
            pltpu.SemaphoreType.DMA((count,)),
            pltpu.SemaphoreType.DMA((count,)),
            pltpu.SemaphoreType.DMA,
            pltpu.SemaphoreType.DMA,
            pltpu.SemaphoreType.DMA((cols // tile,)),
            pltpu.SemaphoreType.DMA((cols // tile,)),
        ],
        compiler_params=pltpu.CompilerParams(
            vmem_limit_bytes=48 << 20, collective_id=1, has_side_effects=True
        ),
        cost_estimate=pl.CostEstimate(
            flops=2 * rows * wide * features, bytes_accessed=20 << 20, transcendentals=0
        ),
    )(grad_packed, whole, terms)
    flat = sums.transpose(1, 0, 2)
    return (
        grad_tokens,
        flat[:, :, :width].reshape(rank, features),
        flat[:, :, width:].reshape(rank, wide),
    )


MESH = pl.DeviceIdType.MESH
PIECES = 8


def gather_kernel(
    outer, shard_ref, out_ref, z_send, z_recv, y_send, y_recv, x_send, x_recv, local_sem
):
    me = lax.axis_index("ctx")
    x = lax.axis_index("groups")
    z, y = me // 2, lax.rem(me, 2)
    rows = shard_ref.shape[0]
    piece = rows // PIECES
    half = piece // 2
    last = outer - 2
    steps = outer - 1

    def ctx_of(line, pair):
        return {"ctx": line * 2 + pair}

    def span(line, pair, start, size):
        return pl.ds(pl.multiple_of((line * 2 + pair) * rows + start, half), size)

    def part(p, side):
        return p * piece + side * half

    def copy(src, dst, send, recv, device):
        return pltpu.make_async_remote_copy(
            src_ref=src, dst_ref=dst, send_sem=send, recv_sem=recv, device_id=device, device_id_type=MESH
        )

    def z_range(k, p):
        return (part(p, x), half) if k == last else (p * piece, piece)

    def z_out(way, k, p):
        step = 1 - 2 * way
        start, size = z_range(k, p)
        place = span(z - step * k, y, start, size)
        src = out_ref.at[place] if k else shard_ref.at[pl.ds(pl.multiple_of(start, half), size)]
        return copy(
            src, out_ref.at[place], z_send.at[way, k, p], z_recv.at[way, k, p], ctx_of(z + step, y)
        )

    def z_in(way, k, p):
        step = 1 - 2 * way
        start, size = z_range(k, p)
        place = out_ref.at[span(z - step * (k + 1), y, start, size)]
        return copy(place, place, z_send.at[way, k, p], z_recv.at[way, k, p], ctx_of(z - step, y))

    def sends(way, k):
        return (z < steps) & (z >= k) if way == 0 else (z > 0) & (z + k <= steps)

    def receives(way, k):
        return z > k if way == 0 else z + k < steps

    def line_of(i):
        if i == 0:
            return z
        way, k = (i - 1) // steps, (i - 1) % steps
        return z - (1 - 2 * way) * (k + 1)

    def item(way, k):
        return 1 + way * steps + k

    def y_out(i, p):
        start = part(p, x)
        place = span(line_of(i), y, start, half)
        src = out_ref.at[place] if i else shard_ref.at[pl.ds(pl.multiple_of(start, half), half)]
        return copy(src, out_ref.at[place], y_send.at[i, p], y_recv.at[i, p], ctx_of(z, 1 - y))

    def y_in(i, p):
        place = out_ref.at[span(line_of(i), 1 - y, part(p, x), half)]
        return copy(place, place, y_send.at[i, p], y_recv.at[i, p], ctx_of(z, 1 - y))

    def x_copy(i, p, side):
        if i > 2 * steps:
            line, pair = line_of(item(i - 2 * steps - 1, last)), y
        else:
            line, pair = line_of(i), 1 - y
        place = out_ref.at[span(line, pair, part(p, side), half)]
        return copy(place, place, x_send.at[i, p], x_recv.at[i, p], {"groups": 1 - x})

    def extra(way):
        return 2 * steps + 1 + way

    barrier = pltpu.get_barrier_semaphore()
    pl.semaphore_signal(barrier, inc=1, device_id=ctx_of(z, 1 - y), device_id_type=MESH)
    pl.semaphore_signal(barrier, inc=1, device_id={"groups": 1 - x}, device_id_type=MESH)
    for step in (1, outer - 1):
        pl.semaphore_signal(
            barrier, inc=1, device_id=ctx_of(lax.rem(z + step, outer), y), device_id_type=MESH
        )
    pl.semaphore_wait(barrier, 4)

    @pl.loop(0, PIECES)
    def _(p):
        for way in range(2):
            @pl.when(sends(way, 0))
            def _():
                z_out(way, 0, p).start()
        y_out(0, p).start()

    own = pltpu.make_async_copy(
        shard_ref, out_ref.at[pl.ds(pl.multiple_of(me * rows, rows), rows)], local_sem
    )
    own.start()

    def pass_on(k, p):
        for way in range(2):
            @pl.when(receives(way, k))
            def _():
                i = item(way, k)
                y_in(i, p).wait_recv()
                x_copy(i, p, x).start()

    for k in range(steps):
        @pl.loop(0, PIECES)
        def _(p):
            for way in range(2):
                @pl.when(receives(way, k))
                def _():
                    z_in(way, k, p).wait_recv()
                    if k < last:
                        @pl.when(sends(way, k + 1))
                        def _():
                            z_out(way, k + 1, p).start()
                    y_out(item(way, k), p).start()
                    if k == last:
                        x_copy(extra(way), p, x).start()
            if k == 0:
                y_in(0, p).wait_recv()
                x_copy(0, p, x).start()

            @pl.when(p > 0)
            def _():
                pass_on(k, p - 1)

            if k > 0:
                @pl.when(p == 0)
                def _():
                    pass_on(k - 1, PIECES - 1)

    pass_on(last, PIECES - 1)
    own.wait()

    @pl.loop(0, PIECES)
    def _(p):
        x_copy(0, p, 1 - x).wait_recv()
        x_copy(0, p, x).wait_send()
        y_out(0, p).wait_send()
        for way in range(2):
            for k in range(steps):
                @pl.when(sends(way, k))
                def _():
                    z_out(way, k, p).wait_send()

                @pl.when(receives(way, k))
                def _():
                    i = item(way, k)
                    x_copy(i, p, 1 - x).wait_recv()
                    x_copy(i, p, x).wait_send()
                    y_out(i, p).wait_send()
                    if k == last:
                        x_copy(extra(way), p, 1 - x).wait_recv()
                        x_copy(extra(way), p, x).wait_send()


def gather(merged, count):
    rows, wide = merged.shape
    outer = count // 2
    items = 2 * (outer - 1) + 1
    dma = pltpu.SemaphoreType.DMA
    hbm = pl.BlockSpec(memory_space=pl.ANY)
    return pl.pallas_call(
        functools.partial(gather_kernel, outer),
        out_shape=jax.ShapeDtypeStruct((rows * count, wide), merged.dtype),
        in_specs=[hbm],
        out_specs=hbm,
        scratch_shapes=[
            dma((2, outer - 1, PIECES)),
            dma((2, outer - 1, PIECES)),
            dma((items, PIECES)),
            dma((items, PIECES)),
            dma((items + 2, PIECES)),
            dma((items + 2, PIECES)),
            dma,
        ],
        compiler_params=pltpu.CompilerParams(collective_id=2, has_side_effects=True),
        cost_estimate=pl.CostEstimate(flops=0, bytes_accessed=300 << 20, transcendentals=0),
    )(merged)


def body(tokens, weight, adapter_a, adapter_b, short_filter, long_filter, skip_gain, cotangent):
    row_count = tokens.shape[0]
    share_rows = weight.shape[0]
    channels = weight.shape[2]
    features = tokens.shape[1]
    adapter_rank = adapter_a.shape[1]
    halo = long_filter.shape[0] + BLOCK
    count = lax.axis_size("ctx")
    seq_total = row_count * count
    first_row = lax.axis_index("ctx") * share_rows
    before = shifted(tokens[row_count - halo :], "ctx", 1)
    after = shifted(tokens[:halo], "ctx", -1)
    cot_after = shifted(cotangent[:halo], "ctx", -1)
    tokens_ext = jnp.concatenate([before, tokens, after], axis=0)
    cot_ext = jnp.concatenate([cotangent, cot_after], axis=0)
    own_rows = lax.dynamic_slice_in_dim(adapter_a, first_row, share_rows, 0)
    flat_b = adapter_b.reshape(adapter_rank, 3 * channels)
    delta_w = jnp.dot(own_rows, flat_b, preferred_element_type=jnp.float32)
    merged = (
        weight.reshape(share_rows, 3 * channels).astype(jnp.float32) + adapter_scale * delta_w
    ).astype(jnp.bfloat16)
    if count == 8 and lax.axis_size("groups") == 2:
        whole = gather(merged, count)
    else:
        whole = lax.all_gather(merged, "ctx", axis=0, tiled=True)
    packed = jnp.dot(tokens_ext, whole, preferred_element_type=jnp.float32).astype(jnp.bfloat16)
    mixed, grad_packed = mixer(
        packed, cot_ext, short_filter, long_filter, skip_gain, row_count, halo
    )
    projected = jnp.dot(tokens, adapter_a, preferred_element_type=jnp.float32).astype(jnp.bfloat16)
    part_b = lax.dot_general(
        projected, grad_packed, (((0,), (0,)), ((), ())), preferred_element_type=jnp.float32
    )
    through = lax.dot_general(
        flat_b, grad_packed, (((1,), (1,)), ((), ())), preferred_element_type=jnp.float32
    ).astype(jnp.bfloat16)
    part_a = jnp.dot(through, tokens, preferred_element_type=jnp.float32)
    if features % (LANES * count) == 0 and (3 * channels) % (LANES * count) == 0:
        grad_tokens, sum_a, sum_b = finish(grad_packed, whole, part_a, part_b, count)
    else:
        sum_a = lax.psum(part_a, ("ctx", "tp"))
        sum_b = lax.psum(part_b, "ctx")
        partial_grad = lax.dot_general(
            grad_packed, whole, (((1,), (1,)), ((), ())), preferred_element_type=jnp.float32
        )
        grad_tokens = lax.psum_scatter(
            partial_grad.astype(jnp.bfloat16), "tp", scatter_dimension=1, tiled=True
        )
    sum_a = sum_a.T
    factor = adapter_scale / math.sqrt(seq_total)
    return (mixed, grad_tokens, sum_a * factor, (sum_b * factor).reshape(adapter_rank, 3, channels))


def solution(mesh):
    return jax.shard_map(
        body,
        mesh=mesh,
        in_specs=(
            P(("groups", "ctx"), None),
            P("ctx", None, "tp"),
            P(),
            P(None, None, "tp"),
            P(None, None, "tp"),
            P(None, "tp"),
            P("tp"),
            P(("groups", "ctx"), "tp"),
        ),
        out_specs=(
            P(("groups", "ctx"), "tp"),
            P(("groups", "ctx"), "tp"),
            P("groups", None),
            P("groups", None, "tp"),
        ),
        check_vma=False,
    )
```

```python
import functools
import math

import jax
import jax.numpy as jnp
from jax import lax
from jax.experimental import pallas as pl
from jax.experimental.pallas import tpu as pltpu
from jax.sharding import PartitionSpec as P

adapter_scale = 0.03125
LANES = 128
SUB = 8
BLOCK = 16
CHUNK = 32


def shifted(value, axis, steps):
    count = lax.axis_size(axis)
    initial, last = (max(0, -steps), min(count, count - steps))
    return lax.ppermute(value, axis, [(source, source + steps) for source in range(initial, last)])


def tiles(ref, first, count):
    start = first * SUB
    if not isinstance(start, int):
        start = pl.multiple_of(start, SUB)
    return ref[pl.ds(start, count * SUB), :].reshape(count, SUB, LANES)


def put(ref, first, value):
    count = value.shape[0]
    ref[pl.ds(pl.multiple_of(first * SUB, SUB), count * SUB), :] = value.reshape(count * SUB, LANES)


def rounded(value):
    return value.astype(jnp.bfloat16).astype(jnp.float32)


def mixer_kernel(
    rows, halo, packed_ref, cot_ref, short_ref, long_ref, skip_ref, mixed_ref, grad_ref,
    p0, p1, p2, cot, query, keyed, valued, gated, gradf,
):
    channels = SUB * LANES
    short_taps = short_ref.shape[0] // 3
    long_taps = long_ref.shape[0]
    spread = (p0, p1, p2)
    front = halo - long_taps

    @pl.loop(0, (rows + 2 * halo) // BLOCK)
    def _(i):
        at = pl.multiple_of(i * BLOCK, BLOCK)
        for g in range(3):
            for s in range(SUB):
                piece = packed_ref[pl.ds(at, BLOCK), pl.ds(g * channels + s * LANES, LANES)]
                spread[g][pl.ds(at * SUB + s, BLOCK, stride=SUB), :] = piece.astype(jnp.float32)

    @pl.loop(0, (rows + halo) // BLOCK)
    def _(i):
        at = pl.multiple_of(i * BLOCK, BLOCK)
        for s in range(SUB):
            piece = cot_ref[pl.ds(at, BLOCK), pl.ds(s * LANES, LANES)]
            cot[pl.ds(at * SUB + s, BLOCK, stride=SUB), :] = piece.astype(jnp.float32)

    def short(ref, g, first, sign):
        total = None
        for j in range(short_taps):
            term = short_ref[j * 3 + g][None] * tiles(ref, first + sign * j, SUB)
            total = term if total is None else total + term
        return total

    @pl.loop(0, (rows + BLOCK + long_taps) // SUB)
    def _(i):
        at = i * SUB
        key = short(p1, 1, at + front, -1)
        val = short(p2, 2, at + front, -1)
        put(keyed, at, key)
        put(valued, at, val)
        put(gated, at, rounded(key * val))

    @pl.loop(0, (rows + halo) // SUB)
    def _(i):
        at = i * SUB
        que = short(p0, 0, at + halo, -1)
        put(query, at, que)
        put(gradf, at, rounded(que * tiles(cot, at, SUB)))

    zero = tuple(jnp.zeros((SUB, LANES), jnp.float32) for _ in range(BLOCK))

    def long_sum(ref, base, sign):
        def chunk(c, acc):
            acc = list(acc)
            tap0 = c * CHUNK
            origin = base + sign * tap0
            low = origin - (CHUNK - 1) if sign < 0 else origin
            seen = {}

            def at(k):
                if k not in seen:
                    seen[k] = ref[pl.ds(pl.multiple_of((low + k) * SUB, SUB), SUB), :]
                return seen[k]

            for j in range(CHUNK):
                tap = long_ref[tap0 + j]
                for i in range(BLOCK):
                    k = i + (CHUNK - 1) - j if sign < 0 else i + j
                    acc[i] = acc[i] + tap * at(k)
            return tuple(acc)

        return lax.fori_loop(0, long_taps // CHUNK, chunk, zero)

    @pl.loop(0, (rows + BLOCK) // BLOCK)
    def _(b):
        at = b * BLOCK
        skip = skip_ref[...]
        ahead = jnp.stack(long_sum(gated, at + long_taps, -1))
        filtered = ahead + skip[None] * tiles(gated, at + long_taps, BLOCK)
        back = jnp.stack(long_sum(gradf, at, 1))
        grad_gated = back + skip[None] * tiles(gradf, at, BLOCK)
        put(p0, at, rounded(tiles(cot, at, BLOCK) * filtered))
        put(p1, at, rounded(grad_gated * tiles(valued, at + long_taps, BLOCK)))
        put(p2, at, rounded(grad_gated * tiles(keyed, at + long_taps, BLOCK)))
        put(gated, at, tiles(query, at, BLOCK) * filtered)

    results = (query, keyed, valued)

    @pl.loop(0, rows // SUB)
    def _(i):
        at = i * SUB
        for g in range(3):
            put(results[g], at, short(spread[g], g, at, 1))

    @pl.loop(0, rows // BLOCK)
    def _(i):
        at = pl.multiple_of(i * BLOCK, BLOCK)
        for s in range(SUB):
            pick = pl.ds(at * SUB + s, BLOCK, stride=SUB)
            mixed_ref[pl.ds(at, BLOCK), pl.ds(s * LANES, LANES)] = gated[pick, :].astype(jnp.bfloat16)
            for g in range(3):
                grad_ref[pl.ds(at, BLOCK), pl.ds(g * channels + s * LANES, LANES)] = results[g][
                    pick, :
                ].astype(jnp.bfloat16)


def mixer(packed, cot, short_filter, long_filter, skip_gain, rows, halo):
    channels = long_filter.shape[1]
    long_taps = long_filter.shape[0]
    full = (rows + 2 * halo) * SUB
    side = (rows + halo) * SUB
    scratch = [pltpu.VMEM((full, LANES), jnp.float32)] * 3 + [
        pltpu.VMEM((side, LANES), jnp.float32)
    ] * 6
    return pl.pallas_call(
        functools.partial(mixer_kernel, rows, halo),
        out_shape=(
            jax.ShapeDtypeStruct((rows, channels), jnp.bfloat16),
            jax.ShapeDtypeStruct((rows, 3 * channels), jnp.bfloat16),
        ),
        in_specs=[pl.BlockSpec(memory_space=pltpu.VMEM)] * 5,
        out_specs=(pl.BlockSpec(memory_space=pltpu.VMEM),) * 2,
        scratch_shapes=scratch,
        compiler_params=pltpu.CompilerParams(vmem_limit_bytes=52 << 20),
        cost_estimate=pl.CostEstimate(
            flops=4 * rows * channels * (long_taps + 42), bytes_accessed=12 << 20, transcendentals=0
        ),
    )(
        packed,
        cot,
        short_filter.reshape(-1, SUB, LANES),
        long_filter.reshape(long_taps, SUB, LANES),
        skip_gain.reshape(SUB, LANES),
    )


def finish_kernel(
    count, grad_ref, whole_ref, terms_ref, tokens_ref, sums_ref,
    held, total, mate, summed, ready, landed,
    send_one, recv_one, send_two, recv_two, send_tp, recv_tp, send_tok, recv_tok,
):
    me = lax.axis_index("ctx")
    mine = lax.axis_index("tp")
    other = 1 - mine
    width = mate.shape[1]
    cols = tokens_ref.shape[1]
    tile = ready.shape[2]
    steps = cols // tile

    barrier = pltpu.get_barrier_semaphore()
    for d in range(1, count):
        pl.semaphore_signal(
            barrier, inc=1, device_id={"ctx": lax.rem(me + d, count)}, device_id_type=pl.DeviceIdType.MESH
        )
    pl.semaphore_signal(barrier, inc=1, device_id={"tp": other}, device_id_type=pl.DeviceIdType.MESH)
    pl.semaphore_wait(barrier, count)

    first = []
    for d in range(1, count):
        peer = lax.rem(me + d, count)
        first.append(
            pltpu.make_async_remote_copy(
                src_ref=terms_ref.at[peer],
                dst_ref=held.at[d],
                send_sem=send_one.at[d],
                recv_sem=recv_one.at[d],
                device_id={"ctx": peer},
                device_id_type=pl.DeviceIdType.MESH,
            )
        )
        first[-1].start()

    def product(half, t):
        at = pl.multiple_of(half * cols + t * tile, tile)
        return lax.dot_general(
            grad_ref[...],
            whole_ref[pl.ds(at, tile), :],
            (((1,), (1,)), ((), ())),
            preferred_element_type=jnp.float32,
        )

    def token_copy(t):
        return pltpu.make_async_remote_copy(
            src_ref=ready.at[t],
            dst_ref=landed.at[t],
            send_sem=send_tok.at[t],
            recv_sem=recv_tok.at[t],
            device_id={"tp": other},
            device_id_type=pl.DeviceIdType.MESH,
        )

    @pl.loop(0, steps)
    def _(t):
        ready[t] = product(other, t).astype(jnp.bfloat16)
        token_copy(t).start()

    own = terms_ref[me]
    for d in range(1, count):
        first[d - 1].wait()
        own = own + held[d]
    total[...] = own
    tp_copy = pltpu.make_async_remote_copy(
        src_ref=total.at[:, pl.ds(0, width)],
        dst_ref=mate,
        send_sem=send_tp,
        recv_sem=recv_tp,
        device_id={"tp": other},
        device_id_type=pl.DeviceIdType.MESH,
    )
    tp_copy.start()

    def own_tile(t):
        value = product(mine, t)
        token_copy(t).wait()
        at = pl.multiple_of(t * tile, tile)
        tokens_ref[:, pl.ds(at, tile)] = (value + landed[t].astype(jnp.float32)).astype(jnp.bfloat16)

    pl.loop(0, steps // 4)(own_tile)
    tp_copy.wait()
    total[:, pl.ds(0, width)] = total[:, pl.ds(0, width)] + mate[...]
    summed[me] = total[...]
    second = []
    for d in range(1, count):
        second.append(
            pltpu.make_async_remote_copy(
                src_ref=total,
                dst_ref=summed.at[me],
                send_sem=send_two.at[d],
                recv_sem=recv_two.at[d],
                device_id={"ctx": lax.rem(me + d, count)},
                device_id_type=pl.DeviceIdType.MESH,
            )
        )
        second[-1].start()
    pl.loop(steps // 4, steps)(own_tile)
    for copy in second:
        copy.wait()
    sums_ref[...] = summed[...]


def finish(grad_packed, whole, part_a, part_b, count):
    rank, features = part_a.shape
    rows, wide = grad_packed.shape
    width, rest = features // count, wide // count
    cols = features // 2
    tile = 256
    terms = jnp.concatenate(
        [part_a.reshape(rank, count, width), part_b.reshape(rank, count, rest)], axis=2
    ).transpose(1, 0, 2)
    vmem = pl.BlockSpec(memory_space=pltpu.VMEM)
    grad_tokens, sums = pl.pallas_call(
        functools.partial(finish_kernel, count),
        out_shape=(
            jax.ShapeDtypeStruct((rows, cols), jnp.bfloat16),
            jax.ShapeDtypeStruct(terms.shape, jnp.float32),
        ),
        in_specs=[vmem] * 3,
        out_specs=(vmem, vmem),
        scratch_shapes=[
            pltpu.VMEM(terms.shape, jnp.float32),
            pltpu.VMEM((rank, width + rest), jnp.float32),
            pltpu.VMEM((rank, width), jnp.float32),
            pltpu.VMEM(terms.shape, jnp.float32),
            pltpu.VMEM((cols // tile, rows, tile), jnp.bfloat16),
            pltpu.VMEM((cols // tile, rows, tile), jnp.bfloat16),
            pltpu.SemaphoreType.DMA((count,)),
            pltpu.SemaphoreType.DMA((count,)),
            pltpu.SemaphoreType.DMA((count,)),
            pltpu.SemaphoreType.DMA((count,)),
            pltpu.SemaphoreType.DMA,
            pltpu.SemaphoreType.DMA,
            pltpu.SemaphoreType.DMA((cols // tile,)),
            pltpu.SemaphoreType.DMA((cols // tile,)),
        ],
        compiler_params=pltpu.CompilerParams(
            vmem_limit_bytes=48 << 20, collective_id=1, has_side_effects=True
        ),
        cost_estimate=pl.CostEstimate(
            flops=2 * rows * wide * features, bytes_accessed=20 << 20, transcendentals=0
        ),
    )(grad_packed, whole, terms)
    flat = sums.transpose(1, 0, 2)
    return (
        grad_tokens,
        flat[:, :, :width].reshape(rank, features),
        flat[:, :, width:].reshape(rank, wide),
    )


MESH = pl.DeviceIdType.MESH
PIECES = 4


def gather_kernel(
    outer, halo, shard_ref, tok_ref, cot_ref, zero_ref, out_ref, tok_out, cot_out,
    z_send, z_recv, y_send, y_recv, x_send, x_recv, local_sem, h_send, h_recv, h_zero, h_own,
):
    me = lax.axis_index("ctx")
    x = lax.axis_index("groups")
    z, y = me // 2, lax.rem(me, 2)
    rows = shard_ref.shape[0]
    piece = rows // PIECES
    half = piece // 2
    last = outer - 2
    steps = outer - 1

    def ctx_of(line, pair):
        return {"ctx": line * 2 + pair}

    def span(line, pair, start, size):
        return pl.ds(pl.multiple_of((line * 2 + pair) * rows + start, half), size)

    def part(p, side):
        return p * piece + side * half

    def copy(src, dst, send, recv, device):
        return pltpu.make_async_remote_copy(
            src_ref=src, dst_ref=dst, send_sem=send, recv_sem=recv, device_id=device, device_id_type=MESH
        )

    def z_range(k, p):
        return (part(p, x), half) if k == last else (p * piece, piece)

    def z_out(way, k, p):
        step = 1 - 2 * way
        start, size = z_range(k, p)
        place = span(z - step * k, y, start, size)
        src = out_ref.at[place] if k else shard_ref.at[pl.ds(pl.multiple_of(start, half), size)]
        return copy(
            src, out_ref.at[place], z_send.at[way, k, p], z_recv.at[way, k, p], ctx_of(z + step, y)
        )

    def z_in(way, k, p):
        step = 1 - 2 * way
        start, size = z_range(k, p)
        place = out_ref.at[span(z - step * (k + 1), y, start, size)]
        return copy(place, place, z_send.at[way, k, p], z_recv.at[way, k, p], ctx_of(z - step, y))

    def sends(way, k):
        return (z < steps) & (z >= k) if way == 0 else (z > 0) & (z + k <= steps)

    def receives(way, k):
        return z > k if way == 0 else z + k < steps

    def line_of(i):
        if i == 0:
            return z
        way, k = (i - 1) // steps, (i - 1) % steps
        return z - (1 - 2 * way) * (k + 1)

    def item(way, k):
        return 1 + way * steps + k

    def y_out(i, p):
        start = part(p, x)
        place = span(line_of(i), y, start, half)
        src = out_ref.at[place] if i else shard_ref.at[pl.ds(pl.multiple_of(start, half), half)]
        return copy(src, out_ref.at[place], y_send.at[i, p], y_recv.at[i, p], ctx_of(z, 1 - y))

    def y_in(i, p):
        place = out_ref.at[span(line_of(i), 1 - y, part(p, x), half)]
        return copy(place, place, y_send.at[i, p], y_recv.at[i, p], ctx_of(z, 1 - y))

    def x_copy(i, p, side):
        if i > 2 * steps:
            line, pair = line_of(item(i - 2 * steps - 1, last)), y
        else:
            line, pair = line_of(i), 1 - y
        place = out_ref.at[span(line, pair, part(p, side), half)]
        return copy(place, place, x_send.at[i, p], x_recv.at[i, p], {"groups": 1 - x})

    def extra(way):
        return 2 * steps + 1 + way

    barrier = pltpu.get_barrier_semaphore()
    pl.semaphore_signal(barrier, inc=1, device_id=ctx_of(z, 1 - y), device_id_type=MESH)
    pl.semaphore_signal(barrier, inc=1, device_id={"groups": 1 - x}, device_id_type=MESH)
    for step in (1, outer - 1):
        pl.semaphore_signal(
            barrier, inc=1, device_id=ctx_of(lax.rem(z + step, outer), y), device_id_type=MESH
        )
    for step in (1, 2 * outer - 1):
        pl.semaphore_signal(
            barrier, inc=1, device_id={"ctx": lax.rem(me + step, 2 * outer)}, device_id_type=MESH
        )
    pl.semaphore_wait(barrier, 6)

    @pl.loop(0, PIECES)
    def _(p):
        for way in range(2):
            @pl.when(sends(way, 0))
            def _():
                z_out(way, 0, p).start()
        y_out(0, p).start()

    own = pltpu.make_async_copy(
        shard_ref, out_ref.at[pl.ds(pl.multiple_of(me * rows, rows), rows)], local_sem
    )
    own.start()

    count, size, cols = 2 * outer, tok_ref.shape[0], cot_ref.shape[1]
    head, tail = pl.ds(0, halo), pl.ds(size - halo, halo)
    spots = (
        (tok_ref.at[tail], tok_out.at[head], zero_ref, 1),
        (tok_ref.at[head], tok_out.at[pl.ds(size + halo, halo)], zero_ref, -1),
        (cot_ref.at[head], cot_out.at[pl.ds(size, halo)], zero_ref.at[:, pl.ds(0, cols)], -1),
    )
    placed = [
        pltpu.make_async_copy(tok_ref, tok_out.at[pl.ds(halo, size)], h_own.at[0]),
        pltpu.make_async_copy(cot_ref, cot_out.at[pl.ds(0, size)], h_own.at[1]),
    ]
    halos, blanks = [], []
    for n, (src, dst, blank, step) in enumerate(spots):
        halos.append(copy(src, dst, h_send.at[n], h_recv.at[n], {"ctx": me + step}))
        blanks.append(pltpu.make_async_copy(blank, dst, h_zero.at[n]))

    def has_target(n):
        return me < count - 1 if spots[n][3] > 0 else me > 0

    def has_source(n):
        return me > 0 if spots[n][3] > 0 else me < count - 1

    for n in range(3):
        @pl.when(has_target(n))
        def _():
            halos[n].start()

        @pl.when(jnp.logical_not(has_source(n)))
        def _():
            blanks[n].start()
    for one in placed:
        one.start()

    def pass_on(k, p):
        for way in range(2):
            @pl.when(receives(way, k))
            def _():
                i = item(way, k)
                y_in(i, p).wait_recv()
                x_copy(i, p, x).start()

    for k in range(steps):
        @pl.loop(0, PIECES)
        def _(p):
            for way in range(2):
                @pl.when(receives(way, k))
                def _():
                    z_in(way, k, p).wait_recv()
                    if k < last:
                        @pl.when(sends(way, k + 1))
                        def _():
                            z_out(way, k + 1, p).start()
                    y_out(item(way, k), p).start()
                    if k == last:
                        x_copy(extra(way), p, x).start()
            if k == 0:
                y_in(0, p).wait_recv()
                x_copy(0, p, x).start()

            @pl.when(p > 0)
            def _():
                pass_on(k, p - 1)

            if k > 0:
                @pl.when(p == 0)
                def _():
                    pass_on(k - 1, PIECES - 1)

    pass_on(last, PIECES - 1)
    own.wait()
    for one in placed:
        one.wait()
    for n in range(3):
        @pl.when(has_target(n))
        def _():
            halos[n].wait_send()

        @pl.when(has_source(n))
        def _():
            halos[n].wait_recv()

        @pl.when(jnp.logical_not(has_source(n)))
        def _():
            blanks[n].wait()

    @pl.loop(0, PIECES)
    def _(p):
        x_copy(0, p, 1 - x).wait_recv()
        x_copy(0, p, x).wait_send()
        y_out(0, p).wait_send()
        for way in range(2):
            for k in range(steps):
                @pl.when(sends(way, k))
                def _():
                    z_out(way, k, p).wait_send()

                @pl.when(receives(way, k))
                def _():
                    i = item(way, k)
                    x_copy(i, p, 1 - x).wait_recv()
                    x_copy(i, p, x).wait_send()
                    y_out(i, p).wait_send()
                    if k == last:
                        x_copy(extra(way), p, 1 - x).wait_recv()
                        x_copy(extra(way), p, x).wait_send()


def gather(merged, tokens, cotangent, halo, count):
    rows, wide = merged.shape
    outer = count // 2
    items = 2 * (outer - 1) + 1
    dma = pltpu.SemaphoreType.DMA
    hbm = pl.BlockSpec(memory_space=pl.ANY)
    return pl.pallas_call(
        functools.partial(gather_kernel, outer, halo),
        out_shape=(
            jax.ShapeDtypeStruct((rows * count, wide), merged.dtype),
            jax.ShapeDtypeStruct((tokens.shape[0] + 2 * halo, tokens.shape[1]), tokens.dtype),
            jax.ShapeDtypeStruct((tokens.shape[0] + halo, cotangent.shape[1]), tokens.dtype),
        ),
        in_specs=[hbm] * 4,
        out_specs=(hbm,) * 3,
        scratch_shapes=[
            dma((2, outer - 1, PIECES)),
            dma((2, outer - 1, PIECES)),
            dma((items, PIECES)),
            dma((items, PIECES)),
            dma((items + 2, PIECES)),
            dma((items + 2, PIECES)),
            dma,
            dma((3,)),
            dma((3,)),
            dma((3,)),
            dma((2,)),
        ],
        compiler_params=pltpu.CompilerParams(collective_id=2, has_side_effects=True),
        cost_estimate=pl.CostEstimate(flops=0, bytes_accessed=300 << 20, transcendentals=0),
    )(merged, tokens, cotangent, jnp.zeros((halo, tokens.shape[1]), tokens.dtype))


def body(tokens, weight, adapter_a, adapter_b, short_filter, long_filter, skip_gain, cotangent):
    row_count = tokens.shape[0]
    share_rows = weight.shape[0]
    channels = weight.shape[2]
    features = tokens.shape[1]
    adapter_rank = adapter_a.shape[1]
    halo = long_filter.shape[0] + BLOCK
    count = lax.axis_size("ctx")
    seq_total = row_count * count
    first_row = lax.axis_index("ctx") * share_rows
    own_rows = lax.dynamic_slice_in_dim(adapter_a, first_row, share_rows, 0)
    flat_b = adapter_b.reshape(adapter_rank, 3 * channels)
    delta_w = jnp.dot(own_rows, flat_b, preferred_element_type=jnp.float32)
    merged = (
        weight.reshape(share_rows, 3 * channels).astype(jnp.float32) + adapter_scale * delta_w
    ).astype(jnp.bfloat16)
    if count == 8 and lax.axis_size("groups") == 2:
        whole, tokens_ext, cot_ext = gather(merged, tokens, cotangent, halo, count)
    else:
        before = shifted(tokens[row_count - halo :], "ctx", 1)
        after = shifted(tokens[:halo], "ctx", -1)
        cot_after = shifted(cotangent[:halo], "ctx", -1)
        tokens_ext = jnp.concatenate([before, tokens, after], axis=0)
        cot_ext = jnp.concatenate([cotangent, cot_after], axis=0)
        whole = lax.all_gather(merged, "ctx", axis=0, tiled=True)
    packed = jnp.dot(tokens_ext, whole, preferred_element_type=jnp.float32).astype(jnp.bfloat16)
    mixed, grad_packed = mixer(
        packed, cot_ext, short_filter, long_filter, skip_gain, row_count, halo
    )
    projected = jnp.dot(tokens, adapter_a, preferred_element_type=jnp.float32).astype(jnp.bfloat16)
    part_b = lax.dot_general(
        projected, grad_packed, (((0,), (0,)), ((), ())), preferred_element_type=jnp.float32
    )
    through = lax.dot_general(
        flat_b, grad_packed, (((1,), (1,)), ((), ())), preferred_element_type=jnp.float32
    ).astype(jnp.bfloat16)
    part_a = jnp.dot(through, tokens, preferred_element_type=jnp.float32)
    if features % (LANES * count) == 0 and (3 * channels) % (LANES * count) == 0:
        grad_tokens, sum_a, sum_b = finish(grad_packed, whole, part_a, part_b, count)
    else:
        sum_a = lax.psum(part_a, ("ctx", "tp"))
        sum_b = lax.psum(part_b, "ctx")
        partial_grad = lax.dot_general(
            grad_packed, whole, (((1,), (1,)), ((), ())), preferred_element_type=jnp.float32
        )
        grad_tokens = lax.psum_scatter(
            partial_grad.astype(jnp.bfloat16), "tp", scatter_dimension=1, tiled=True
        )
    sum_a = sum_a.T
    factor = adapter_scale / math.sqrt(seq_total)
    return (mixed, grad_tokens, sum_a * factor, (sum_b * factor).reshape(adapter_rank, 3, channels))


def solution(mesh):
    return jax.shard_map(
        body,
        mesh=mesh,
        in_specs=(
            P(("groups", "ctx"), None),
            P("ctx", None, "tp"),
            P(),
            P(None, None, "tp"),
            P(None, None, "tp"),
            P(None, "tp"),
            P("tp"),
            P(("groups", "ctx"), "tp"),
        ),
        out_specs=(
            P(("groups", "ctx"), "tp"),
            P(("groups", "ctx"), "tp"),
            P("groups", None),
            P("groups", None, "tp"),
        ),
        check_vma=False,
    )
```
